128 devices in a mesh: gx: 8 (over z, core), gy: 16 (over x, y).
Axes of the slice: x: 4, y: 4, z: 4, core: 2. Of those that a mesh axis runs over, the one named last changes fastest.
Arguments:
- state: float32 [100, 524288], P(None, ('gx', 'gy')), may hold values from -6 to 6
- adjoint: float32 [175, 524288], P(None, ('gx', 'gy')), may hold values from -6 to 6
- geometry: float32 [60, 524288], P(None, ('gx', 'gy')), may hold values from -6 to 6
- face_blocks: float32 [75, 1048576], P(None, ('gx', 'gy')), may hold values from -6 to 6
- face_elem: int32 [1048576], P(('gx', 'gy')), may hold values from 0 to 4095, as said below
- move_ids: int32 [512, 1024], P(('gx', 'gy')), may hold values from 0 to 4095, as said below
- move_counts: int32 [512], P(('gx', 'gy')), may hold values from 0 to 1024, as said below
- basis: float32 [46, 20], replicated, may hold values from -1.25 to 1.25
- geo_grad: float32 [3, 46, 20], replicated, may hold values from -1.25 to 1.25
- test_grad: float32 [35, 138], replicated, may hold values from -0.5 to 0.5
- lift: float32 [35, 15], replicated, may hold values from -1.5 to 1.5
- speeds: float32 [3, 5], replicated, may hold values from -1 to 1
Outputs:
- state_out: float32 [100, 1048576], P(None, ('gx', 'gy'))
- adjoint_out: float32 [175, 1048576], P(None, ('gx', 'gy'))
- geometry_out: float32 [60, 1048576], P(None, ('gx', 'gy'))
- faces_out: float32 [75, 2097152], P(None, ('gx', 'gy'))
- residual: float32 [175, 524288], P(None, ('gx', 'gy'))
The draws below stay inside these ranges and needn't reach their ends.
Inputs may be any that keep to these rules, and one draw needn't show every extreme that they name: `move_counts`: entry 4 d + k is how many elements device d sends toward its side k; it is 0 toward a side with no device, and every device sends exactly 1024 elements toward one side. `move_ids`: row 4 d + k lists device d's local element numbers for side k, the first move_counts[4 d + k] of them used; the 4096 numbers of one device are distinct. `face_elem`: every element of a device owns exactly two of the device's faces.
All inputs are finite; a program needn't handle non-finite values.
Results may differ from the reference program's by a relative error of at most 0.0003.
Values sent between devices are 32-bit elements; how exact they have to be, the bound alone decides.
No kernel may reach another device: no remote copies, remote signals or barrier semaphores. Data moves between devices by JAX's collectives and lax.ppermute only.
A program may use at most 128 MiB of HBM per device.

```python
import jax
import jax.numpy as jnp
from jax import lax

NV = 5
NS = 20
NA = 35
NQ = 46
NFT = 15
E_DEV = 4096
CAP = 1024
ELEMS = 524288
FACES = 1048576
N_GX = 8
N_GY = 16


def draw_move_counts(key, part):
    ndev = N_GX * N_GY
    counts = jax.random.randint(key, (ndev, 4), 1, CAP + 1)
    device = jnp.arange(ndev, dtype=jnp.int32)
    row = device // N_GY
    col = device % N_GY
    valid = jnp.stack([row > 0, row < N_GX - 1, col > 0, col < N_GY - 1], 1)
    filled = jnp.where(row < N_GX - 1, 1, 0)
    side = jnp.arange(4, dtype=jnp.int32)[None, :]
    counts = jnp.where(side == filled[:, None], CAP, counts)
    counts = jnp.where(valid, counts, 0)
    return counts.reshape(-1).astype(jnp.int32)


def draw_move_ids(key, part):
    ndev = N_GX * N_GY
    keys = jax.random.split(key, ndev)
    picks = jax.vmap(lambda one: jax.random.permutation(one, E_DEV)[:4 * CAP])(keys)
    return picks.reshape(4 * ndev, CAP).astype(jnp.int32)


def draw_face_elem(key, part):
    ndev = N_GX * N_GY
    keys = jax.random.split(jax.random.fold_in(key, 7), ndev)
    twice = jnp.concatenate([jnp.arange(E_DEV, dtype=jnp.int32), jnp.arange(E_DEV, dtype=jnp.int32)])
    owners = jax.vmap(lambda one: jax.random.permutation(one, twice))(keys)
    return owners.reshape(-1).astype(jnp.int32)


def level_of(key, shape, cuts, smallest, top_value):
    loudness = 1.0
    for position, shards_of in cuts:
        draws = jax.random.uniform(jax.random.fold_in(jax.random.fold_in(key, 6), position), (shards_of,), jnp.float32, smallest / len(cuts), top_value / len(cuts))
        loudness = loudness * jnp.repeat(jnp.exp(draws), shape[position] // shards_of).reshape((-1,) + (1,) * (len(shape) - 1 - position))
    return loudness


def centred(own_key, extent, width, bound, pieces=(), kind=jnp.bfloat16):
    entries = jax.random.normal(own_key, extent, jnp.float32) * width
    if len(pieces) > 0:
        entries = level_of(own_key, extent, pieces, -0.22, 0.18) * entries
    return jnp.clip(entries, min=-bound, max=bound).astype(kind)


def setup_inputs(seed: int = 0) -> dict:
    arg_keys = jax.random.split(jax.random.key(seed), 13)
    state = centred(arg_keys[0], (NV * NS, ELEMS), 1.0, 6.0, ((1, 128),), jnp.float32)
    adjoint = centred(arg_keys[1], (NV * NA, ELEMS), 1.0, 6.0, ((1, 128),), jnp.float32)
    geometry = centred(arg_keys[2], (3 * NS, ELEMS), 1.0, 6.0, ((1, 128),), jnp.float32)
    face_blocks = centred(arg_keys[3], (NV * NFT, FACES), 1.0, 6.0, ((1, 128),), jnp.float32)
    face_elem = draw_face_elem(jax.random.fold_in(arg_keys[12], 71), 0)
    move_ids = draw_move_ids(jax.random.fold_in(arg_keys[12], 71), 0)
    move_counts = draw_move_counts(jax.random.fold_in(arg_keys[12], 71), 0)
    basis = centred(arg_keys[7], (NQ, NS), NS ** -0.5, 1.25, (), jnp.float32)
    geo_grad = centred(arg_keys[8], (3, NQ, NS), NS ** -0.5, 1.25, (), jnp.float32)
    test_grad = centred(arg_keys[9], (NA, 3 * NQ), (3 * NQ) ** -0.5, 0.5, (), jnp.float32)
    lift = centred(arg_keys[10], (NA, NFT), NFT ** -0.5, 1.5, (), jnp.float32)
    speeds = jnp.clip(jax.random.uniform(arg_keys[11], (3, NV), jnp.float32, -1.0, 1.0), -1.0, 1.0)
    return dict(state=state, adjoint=adjoint, geometry=geometry, face_blocks=face_blocks, face_elem=face_elem, move_ids=move_ids, move_counts=move_counts, basis=basis, geo_grad=geo_grad, test_grad=test_grad, lift=lift, speeds=speeds)


def departures(ids, counts, elems):
    cap = ids.shape[1]
    live = (jnp.arange(cap, dtype=jnp.int32)[None, :] < counts[:, None]).astype(jnp.float32)
    departed = jnp.zeros((elems,), jnp.float32).at[ids.reshape(-1)].max(live.reshape(-1))
    return live, 1.0 - departed


def face_pair(blocks, owners, elems):
    nfaces = owners.shape[0]
    where = jnp.arange(nfaces, dtype=jnp.int32)
    first = jnp.full((elems,), nfaces, jnp.int32).at[owners].min(where)
    second = jnp.zeros((elems,), jnp.int32).at[owners].max(where)
    return jnp.take(blocks, first, axis=1), jnp.take(blocks, second, axis=1)


def enriched(field, coords, face_sum, basis, geo_grad, test_grad, lift, speeds):
    high = lax.Precision.HIGHEST
    nq, ns = basis.shape
    na = test_grad.shape[0]
    nv = speeds.shape[1]
    nft = lift.shape[1]
    count = field.shape[1]
    values = jnp.einsum("qs,vse->vqe", basis, field.reshape(nv, ns, count), precision=high)
    jac = jnp.einsum("kqs,cse->ckqe", geo_grad, coords.reshape(3, ns, count), precision=high)
    rows = []
    for c in range(3):
        cols = []
        for k in range(3):
            cols.append(jac[(c + 1) % 3, (k + 1) % 3] * jac[(c + 2) % 3, (k + 2) % 3]
                        - jac[(c + 1) % 3, (k + 2) % 3] * jac[(c + 2) % 3, (k + 1) % 3])
        rows.append(jnp.stack(cols, 0))
    cof = jnp.stack(rows, 0)
    flux = values * (1.0 + 0.5 * jnp.tanh(values))
    weight = jnp.einsum("ckqe,cv->kvqe", cof, speeds, precision=high)
    fhat = weight * flux[None]
    out = jnp.einsum("ikq,kvqe->vie", test_grad.reshape(na, 3, nq), fhat, precision=high)
    out = out + jnp.einsum("if,vfe->vie", lift, face_sum.reshape(nv, nft, count), precision=high)
    return out.reshape(nv * na, count)


def reference(state, adjoint, geometry, face_blocks, face_elem, move_ids, move_counts,
              basis, geo_grad, test_grad, lift, speeds):
    ndev = N_GX * N_GY
    elems = E_DEV
    cap = CAP

    def split(a):
        return a.reshape(a.shape[0], ndev, -1).transpose(1, 0, 2)

    fields = (split(state), split(adjoint), split(geometry), split(face_blocks),
              face_elem.reshape(ndev, -1), move_ids.reshape(ndev, 4, cap), move_counts.reshape(ndev, 4))
    widths = (state.shape[0], adjoint.shape[0], geometry.shape[0], face_blocks.shape[0])

    def pack(items):
        st, ad, ge, fb, owners, ids, counts = items
        live, keep = departures(ids, counts, elems)
        first, second = face_pair(fb, owners, elems)
        record = jnp.concatenate([st, ad, ge, first, second], 0)
        sent = jnp.take(record, ids, axis=1) * live[None]
        face_keep = keep[owners]
        kept = jnp.concatenate([st * keep, ad * keep, ge * keep], 0)
        return sent, kept, fb * face_keep

    sent, kept, kept_faces = lax.map(pack, fields)
    rec = sent.shape[1]
    grid = sent.reshape(N_GX, N_GY, rec, 4, cap)
    zero_row = jnp.zeros((1, N_GY, rec, cap), jnp.float32)
    zero_col = jnp.zeros((N_GX, 1, rec, cap), jnp.float32)
    from_low_row = jnp.concatenate([zero_row, grid[:-1, :, :, 1]], 0)
    from_high_row = jnp.concatenate([grid[1:, :, :, 0], zero_row], 0)
    from_low_col = jnp.concatenate([zero_col, grid[:, :-1, :, 3]], 1)
    from_high_col = jnp.concatenate([grid[:, 1:, :, 2], zero_col], 1)
    arrived = jnp.concatenate([from_low_row, from_high_row, from_low_col, from_high_col], 3)
    arrived = arrived.reshape(ndev, rec, 4 * cap)
    w0, w1, w2, w3 = widths
    a_state = arrived[:, :w0]
    a_adj = arrived[:, w0:w0 + w1]
    a_geo = arrived[:, w0 + w1:w0 + w1 + w2]
    a_first = arrived[:, w0 + w1 + w2:w0 + w1 + w2 + w3]
    a_second = arrived[:, w0 + w1 + w2 + w3:]
    new_state = jnp.concatenate([kept[:, :w0], a_state], 2)
    new_adj = jnp.concatenate([kept[:, w0:w0 + w1], a_adj], 2)
    new_geo = jnp.concatenate([kept[:, w0 + w1:], a_geo], 2)
    new_faces = jnp.concatenate([kept_faces, a_first, a_second], 2)

    def residual_of(items):
        st, ge, fs = items
        return enriched(st, ge, fs, basis, geo_grad, test_grad, lift, speeds)

    res = lax.map(residual_of, (a_state, a_geo, a_first + a_second))

    def join(a):
        return a.transpose(1, 0, 2).reshape(a.shape[1], -1)

    return join(new_state), join(new_adj), join(new_geo), join(new_faces), join(res)
```

```python
import functools

import jax
import jax.numpy as jnp
from jax import lax
from jax.experimental import pallas as pl
from jax.experimental.pallas import tpu as pltpu
from jax.sharding import PartitionSpec as P

F32 = jnp.float32
BF16 = jnp.bfloat16
I32 = jnp.int32
VMEM = pltpu.VMEM
L = 128
NV, NS, NA, NQ, NFT = 5, 20, 35, 46, 15
QP = 48
E = 4096
CAP = 1024
RS, RA, RG, RF = NV * NS, NV * NA, 3 * NS, NV * NFT
RSG = RS + RG
VALS = NV * QP
WROWS = VALS + 9 * QP


def spec(space=pltpu.VMEM):
    return pl.BlockSpec(memory_space=space)


ANY = pl.ANY
SMEM = pltpu.SMEM


def params(mib):
    return pltpu.CompilerParams(vmem_limit_bytes=mib << 20)


COST = pl.CostEstimate(flops=1, transcendentals=0, bytes_accessed=1)


def padded(block, rows):
    return jnp.concatenate([block, jnp.zeros((rows - block.shape[0], L), F32)], 0)


def at(c):
    return pl.ds(pl.multiple_of(c * L, L), L)


def copy_rows(ids, row, pairs):
    for j in range(L):
        e = ids[row, j]
        for src, dst in pairs:
            dst[pl.ds(j, 1), :] = src[pl.ds(e, 1), :]


def ids_to_scalar(ids_v, ids, sems, sides):
    copies = []
    for side in sides:
        for b in range(CAP // L):
            r = side * (CAP // L) + b
            copies.append(
                pltpu.make_async_copy(
                    ids_v.at[pl.ds(side, 1), pl.ds(b * L, L)], ids.at[pl.ds(r, 1), :], sems.at[r]
                )
            )
    for c in copies:
        c.start()
    return copies


def live_lanes(cnt, side, block):
    return lax.broadcasted_iota(I32, (1, L), 1) + block * L < cnt[side]


def ids_scratch():
    return [pltpu.SMEM((E // L, L), I32), pltpu.SemaphoreType.DMA((E // L,))]


def pack_loop(ids, cnt, sides, srcs, bufs, emit):
    for s, side in enumerate(sides):

        def two(i, carry, s=s, side=side):
            for h in range(2):
                block = i * 2 + h
                copy_rows(ids, side * (CAP // L) + block, list(zip(srcs, bufs[h])))
                live = live_lanes(cnt, side, block)
                emit(s, block, live, [b[...].T for b in bufs[h]])
            return carry

        lax.fori_loop(0, CAP // L // 2, two, 0)


def sg_first_body(ids_v, cnt, st, ge, up, dn, xs, xg, a0, a1, b0, b1, ids, idsem):
    moved = ids_to_scalar(ids_v, ids, idsem, (2, 3))

    def fwd(c, carry):
        xs[at(c), :] = padded(st[:, at(c)], L).T
        xg[at(c), :] = padded(ge[:, at(c)], L).T
        return carry

    lax.fori_loop(0, E // L, fwd, 0, unroll=2)
    for c in moved:
        c.wait()
    outs = (up, dn)

    def emit(s, block, live, parts):
        outs[s][0:RS, at(block)] = jnp.where(live, parts[0][:RS], 0.0)
        outs[s][RS:RSG, at(block)] = jnp.where(live, parts[1][:RG], 0.0)

    pack_loop(ids, cnt, (3, 2), (xs, xg), ((a0, a1), (b0, b1)), emit)


def sg_first(ids, cnt, st, ge):
    return pl.pallas_call(
        sg_first_body,
        out_shape=[jax.ShapeDtypeStruct((RSG, CAP), F32)] * 2,
        in_specs=[spec(), spec(SMEM), spec(), spec()],
        out_specs=[spec(), spec()],
        scratch_shapes=[VMEM((E, L), F32)] * 2 + [VMEM((L, L), F32)] * 4 + ids_scratch(),
        compiler_params=params(12),
        cost_estimate=COST,
        name="pack_sg_gy",
    )(ids, cnt, st, ge)


def sg_second_body(
    ids_v, cnt, keep, st, ge, up, dn, st_out, ge_out, xs, xg, ks, kg, a0, a1, b0, b1, sems, ids, idsem,
):
    moved = ids_to_scalar(ids_v, ids, idsem, (0, 1))

    def fwd(c, carry):
        k = keep[pl.ds(c, 1), :]
        s, g = st[:, at(c)], ge[:, at(c)]
        ks[:, at(c)] = s * k
        kg[:, at(c)] = g * k
        xs[at(c), :] = padded(s, L).T
        xg[at(c), :] = padded(g, L).T
        return carry

    lax.fori_loop(0, E // L, fwd, 0, unroll=2)
    c0 = pltpu.make_async_copy(ks, st_out.at[:, pl.ds(0, E)], sems.at[0])
    c1 = pltpu.make_async_copy(kg, ge_out.at[:, pl.ds(0, E)], sems.at[1])
    c0.start()
    c1.start()
    for c in moved:
        c.wait()
    outs = (up, dn)

    def emit(s, block, live, parts):
        outs[s][0:RS, at(block)] = jnp.where(live, parts[0][:RS], 0.0)
        outs[s][RS:RSG, at(block)] = jnp.where(live, parts[1][:RG], 0.0)

    pack_loop(ids, cnt, (1, 0), (xs, xg), ((a0, a1), (b0, b1)), emit)
    c0.wait()
    c1.wait()


def sg_second(ids, cnt, keep, st, ge):
    return pl.pallas_call(
        sg_second_body,
        out_shape=[jax.ShapeDtypeStruct((RSG, CAP), F32)] * 2
        + [jax.ShapeDtypeStruct((RS, 2 * E), F32), jax.ShapeDtypeStruct((RG, 2 * E), F32)],
        in_specs=[spec(), spec(SMEM), spec(), spec(), spec()],
        out_specs=[spec(), spec(), spec(ANY), spec(ANY)],
        scratch_shapes=[VMEM((E, L), F32)] * 2
        + [VMEM((RS, E), F32), VMEM((RG, E), F32)]
        + [VMEM((L, L), F32)] * 4
        + [pltpu.SemaphoreType.DMA((2,))]
        + ids_scratch(),
        compiler_params=params(16),
        cost_estimate=COST,
        name="pack_sg_gx",
    )(ids, cnt, keep, st, ge)


def adj_body(
    ids_v, cnt, keep, ad, yu, yd, xu, xd, ad_out, x0, x1, ka, a0, a1, b0, b1, sem, ids, idsem,
):
    moved = ids_to_scalar(ids_v, ids, idsem, range(4))

    def fwd(c, carry):
        k = keep[pl.ds(c, 1), :]
        p, q = ad[0:L, at(c)], ad[L:RA, at(c)]
        ka[0:L, at(c)] = p * k
        ka[L:RA, at(c)] = q * k
        x0[at(c), :] = p.T
        x1[at(c), :] = padded(q, L).T
        return carry

    lax.fori_loop(0, E // L, fwd, 0, unroll=2)
    c0 = pltpu.make_async_copy(ka, ad_out.at[:, pl.ds(0, E)], sem.at[0])
    c0.start()
    for c in moved:
        c.wait()
    outs = (yu, yd, xu, xd)

    def emit(s, block, live, parts):
        outs[s][0:L, at(block)] = jnp.where(live, parts[0], 0.0)
        outs[s][L:RA, at(block)] = jnp.where(live, parts[1][: RA - L], 0.0)

    pack_loop(ids, cnt, (3, 2, 1, 0), (x0, x1), ((a0, a1), (b0, b1)), emit)
    c0.wait()


def adj_pack(ids, cnt, keep, ad):
    return pl.pallas_call(
        adj_body,
        out_shape=[jax.ShapeDtypeStruct((RA, CAP), F32)] * 4
        + [jax.ShapeDtypeStruct((RA, 2 * E), F32)],
        in_specs=[spec(), spec(SMEM), spec(), spec()],
        out_specs=[spec()] * 4 + [spec(ANY)],
        scratch_shapes=[VMEM((E, L), F32)] * 2
        + [VMEM((RA, E), F32)]
        + [VMEM((L, L), F32)] * 4
        + [pltpu.SemaphoreType.DMA((1,))]
        + ids_scratch(),
        compiler_params=params(18),
        cost_estimate=COST,
        name="pack_adj",
    )(ids, cnt, keep, ad)


def dot_nt(a, b):
    return lax.dot_general(a, b, (((1,), (1,)), ((), ())), preferred_element_type=F32)


def dot_nn(a, b):
    return lax.dot_general(a, b, (((1,), (0,)), ((), ())), preferred_element_type=F32)


def faces_body(
    ids_v, owners, cnt, fb, yu, yd, xu, xd, keep, fb_out,
    xf, kf, fkeep, sums, depart, nums, nums_s, a0, a1, b0, b1, sems,
):
    hi32 = lax.broadcasted_iota(I32, (32, L), 0)
    lo128 = lax.broadcasted_iota(I32, (L, L), 0)
    lane = lax.broadcasted_iota(I32, (1, L), 1)
    sq = lane * lane
    weights = [w.astype(F32) for w in (lane, sq >> 7, sq & 127)]
    nf = 2 * E // L
    ne = E // L
    unroll = 4

    def onehots(row):
        mine = hi32 == (row >> 7)
        low = (lo128 == (row & 127)).astype(F32).astype(BF16)
        return mine, low

    sums[...] = jnp.zeros_like(sums)
    depart[...] = jnp.zeros_like(depart)

    def face_sums(g, carry):
        s1, s2 = carry
        for u in range(unroll):
            i = g * unroll + u
            mine, low = onehots(owners[pl.ds(i, 1), :])
            ones = mine.astype(F32)
            left = jnp.concatenate([ones] + [ones * w for w in weights], 0).astype(BF16)
            r = dot_nt(left, low).astype(I32)
            n, l, q = r[0:32], r[32:64], r[64:96] * 128 + r[96:128]
            base = i * L
            s1 = s1 + base * n + l
            s2 = s2 + base * base * n + 2 * base * l + q
        return s1, s2

    zero = jnp.zeros((32, L), I32)
    s1, s2 = lax.fori_loop(0, nf // unroll, face_sums, (zero, zero))
    gap = jnp.floor(jnp.sqrt((2 * s2 - s1 * s1).astype(F32)) + 0.5).astype(I32)
    first, second = (s1 - gap) >> 1, (s1 + gap) >> 1
    table = jnp.concatenate([first >> 7, first & 127, second >> 7, second & 127], 0)
    table = table.astype(F32).astype(BF16)

    def slots(g, dep, side):
        for u in range(unroll):
            b = g * unroll + u
            r = side * (CAP // L) + b
            mine, low = onehots(ids_v[pl.ds(side, 1), at(b)])
            live = (lane + b * L < cnt[side]).astype(F32)
            ones = mine.astype(F32)
            dep = dep + dot_nt((ones * live).astype(BF16), low)
            found = dot_nn(table, low)
            pick = [
                jnp.sum(jnp.where(mine, found[32 * m : 32 * m + 32], 0.0), 0, keepdims=True)
                for m in range(4)
            ]
            nums[pl.ds(r, 1), :] = (pick[0] * 128.0 + pick[1]).astype(I32)
            nums[pl.ds(ne + r, 1), :] = (pick[2] * 128.0 + pick[3]).astype(I32)
        return dep

    dep = jnp.zeros((32, L), F32)
    for side in range(4):
        dep = lax.fori_loop(0, CAP // L // unroll, functools.partial(slots, side=side), dep)
    to_scalar = pltpu.make_async_copy(nums, nums_s, sems.at[1])
    to_scalar.start()
    kept = 1.0 - jnp.minimum(dep, 1.0)
    keep[...] = kept
    kept16 = kept.astype(BF16)

    def fwd(g, carry):
        for u in range(2):
            c = g * 2 + u
            mine, low = onehots(owners[pl.ds(c, 1), :])
            k = jnp.sum(jnp.where(mine, dot_nn(kept16, low), 0.0), 0, keepdims=True)
            f = fb[:, at(c)]
            kf[:, at(c)] = f * k
            xf[at(c), :] = padded(f, L).T
        return carry

    lax.fori_loop(0, nf // 2, fwd, 0)
    c0 = pltpu.make_async_copy(kf, fb_out.at[:, pl.ds(0, 2 * E)], sems.at[0])
    c0.start()
    to_scalar.wait()
    outs = (yu, yd, xu, xd)
    bufs = ((a0, a1), (b0, b1))
    for s, side in enumerate((3, 2, 1, 0)):

        def two(i, carry, s=s, side=side):
            for h in range(2):
                block = i * 2 + h
                row = side * (CAP // L) + block
                copy_rows(nums_s, row, [(xf, bufs[h][0])])
                copy_rows(nums_s, ne + row, [(xf, bufs[h][1])])
                live = live_lanes(cnt, side, block)
                outs[s][0:RF, at(block)] = jnp.where(live, bufs[h][0][...].T[:RF], 0.0)
                outs[s][RF : 2 * RF, at(block)] = jnp.where(live, bufs[h][1][...].T[:RF], 0.0)
            return carry

        lax.fori_loop(0, CAP // L // 2, two, 0)
    c0.wait()


def faces_pack(ids, owners, cnt, fb):
    return pl.pallas_call(
        faces_body,
        out_shape=[jax.ShapeDtypeStruct((2 * RF, CAP), F32)] * 4
        + [jax.ShapeDtypeStruct((32, L), F32), jax.ShapeDtypeStruct((RF, 4 * E), F32)],
        in_specs=[spec(), spec(), spec(SMEM), spec()],
        out_specs=[spec()] * 5 + [spec(ANY)],
        scratch_shapes=[
            VMEM((2 * E, L), F32),
            VMEM((RF, 2 * E), F32),
            VMEM((64, L), F32),
            VMEM((8, L), F32),
            VMEM((8, L), F32),
            VMEM((64, L), I32),
            SMEM((64, L), I32),
        ]
        + [VMEM((L, L), F32)] * 4
        + [pltpu.SemaphoreType.DMA((2,))],
        compiler_params=params(17),
        cost_estimate=COST,
        name="pack_faces",
    )(ids, owners, cnt, fb)


NB = 256


def split(x):
    hi = x.astype(BF16)
    return hi, (x - hi.astype(F32)).astype(BF16)


def arrive_body(
    part, first_call, speeds, basis, grad, test, lift, sg_a, sg_b, fp_a, fp_b, *rest,
):
    if first_call:
        st_in, ge_in, fb_in, st_out, ge_out, fb_out, res_out = rest[:7]
        rest = rest[7:]
    else:
        st_in, ge_in, fb_in, res_in, st_out, ge_out, fb_out, res_out = rest[:8]
        rest = rest[8:]
    wf, w3, tt, lf, ll, vj, fh, ks, kg, k1, k2, kr, sems = rest
    cols = pl.ds(E + part * 2 * CAP, 2 * CAP)

    wf[...] = jnp.zeros_like(wf)
    for v in range(NV):
        wf[v * NS : (v + 1) * NS, v * QP : v * QP + NQ] = basis[...]
    for c in range(3):
        for k in range(3):
            r = VALS + (c * 3 + k) * QP
            wf[RS + c * NS : RS + (c + 1) * NS, r : r + NQ] = grad[k]
    for r in range(0, 768, L):
        top = wf[0:L, r : r + L].T
        low = wf[L : 2 * L, r : r + L].T
        wide = jnp.concatenate([top, low], 1)[: min(L, WROWS - r)]
        wh, wl = split(wide[:, 0:RSG])
        here = slice(r, min(r + L, WROWS))
        w3[here, 0:RSG] = wh
        w3[here, RSG : 2 * RSG] = wh
        w3[here, 2 * RSG : 3 * RSG] = wl
    lf[...] = jnp.zeros_like(lf)
    lf[0:NA, 0 : 3 * QP] = jnp.zeros((NA, 3 * QP), F32)
    for k in range(3):
        lf[0:NA, k * QP : k * QP + NQ] = test[:, k * NQ : (k + 1) * NQ]
    th, tl = split(lf[0:48, 0 : 3 * QP])
    tt[0:48, :] = th
    tt[48:96, :] = tl
    lf[...] = jnp.zeros_like(lf)
    for v in range(NV):
        lf[v * NFT : (v + 1) * NFT, v * 40 : v * 40 + NA] = lift[...]
    lt = jnp.concatenate([lf[0:L, 0:L].T, lf[0:L, L : 2 * L].T], 0)
    lh, l2 = split(lt[0:208, 0:80])
    ll[0:208, :] = lh
    ll[208:416, :] = l2

    def block(b, carry, sg, fp, d):
        src = pl.ds(pl.multiple_of(b * NB, NB), NB)
        dst = pl.ds(pl.multiple_of(d * CAP + b * NB, NB), NB)
        x = sg[:, src]
        ks[:, dst] = x[0:RS]
        kg[:, dst] = x[RS:RSG]
        f1, f2 = fp[0:RF, src], fp[RF : 2 * RF, src]
        k1[:, dst] = f1
        k2[:, dst] = f2
        hi, lo = split(x)
        vj[...] = dot_nn(w3[...], jnp.concatenate([hi, lo, hi], 0))
        for t in range(QP // 16):
            for h in range(NB // L):
                lanes = slice(h * L, (h + 1) * L)

                def part_of(r):
                    return vj[r + 16 * t : r + 16 * t + 16, lanes]

                jac = [[part_of(VALS + (c * 3 + k) * QP) for k in range(3)] for c in range(3)]
                flux = []
                for v in range(NV):
                    u = part_of(v * QP)
                    flux.append(u + u * (0.5 * jnp.tanh(u)))
                for k in range(3):
                    k1_, k2_ = (k + 1) % 3, (k + 2) % 3
                    cof = []
                    for c in range(3):
                        c1, c2 = (c + 1) % 3, (c + 2) % 3
                        cof.append(jac[c1][k1_] * jac[c2][k2_] - jac[c1][k2_] * jac[c2][k1_])
                    for v in range(NV):
                        w = cof[0] * speeds[0, v] + cof[1] * speeds[1, v] + cof[2] * speeds[2, v]
                        fhi, flo = split(w * flux[v])
                        r = k * QP + 16 * t
                        fh[v, 0, r : r + 16, lanes] = fhi
                        fh[v, 1, r : r + 16, lanes] = flo
        fs = jnp.concatenate([f1 + f2, jnp.zeros((80 - RF, NB), F32)], 0)
        shi, slo = split(fs)
        m1 = dot_nn(ll[...], shi)
        lifted = m1[0:208] + m1[208:416] + dot_nn(ll[0:208, :], slo)
        for v in range(NV):
            d1 = dot_nn(tt[...], fh[v, 0])
            d2 = dot_nn(tt[0:48, :], fh[v, 1])
            total = d1[0:40] + d1[48:88] + d2[0:40] + lifted[40 * v : 40 * v + 40]
            kr[NA * v : NA * (v + 1), dst] = total[0:NA]
        return carry

    for d, (sg, fp) in enumerate(((sg_a, fp_a), (sg_b, fp_b))):
        lax.fori_loop(0, CAP // NB, functools.partial(block, sg=sg, fp=fp, d=d), 0)
    copies = (
        (ks, st_out.at[:, cols]),
        (kg, ge_out.at[:, cols]),
        (k1, fb_out.at[:, pl.ds(2 * E + part * 2 * CAP, 2 * CAP)]),
        (k2, fb_out.at[:, pl.ds(3 * E + part * 2 * CAP, 2 * CAP)]),
        (kr, res_out.at[:, pl.ds(part * 2 * CAP, 2 * CAP)]),
    )
    copies = [pltpu.make_async_copy(s, t, sems.at[m]) for m, (s, t) in enumerate(copies)]
    for c in copies:
        c.start()
    for c in copies:
        c.wait()


def arrive(part, weights, pieces, outs):
    speeds, basis, grad, test, lift = weights
    first_call = len(outs) == 3
    shapes = [
        jax.ShapeDtypeStruct((RS, 2 * E), F32),
        jax.ShapeDtypeStruct((RG, 2 * E), F32),
        jax.ShapeDtypeStruct((RF, 4 * E), F32),
        jax.ShapeDtypeStruct((RA, E), F32),
    ]
    return pl.pallas_call(
        functools.partial(arrive_body, part, first_call),
        out_shape=shapes,
        in_specs=[spec(SMEM)] + [spec()] * 8 + [spec(ANY)] * len(outs),
        out_specs=[spec(ANY)] * 4,
        input_output_aliases={9 + i: i for i in range(len(outs))},
        scratch_shapes=[
            VMEM((256, 768), F32),
            VMEM((WROWS, 3 * RSG), BF16),
            VMEM((96, 3 * QP), BF16),
            VMEM((208, 256), F32),
            VMEM((416, 80), BF16),
            VMEM((WROWS, NB), F32),
            VMEM((NV, 2, 3 * QP, NB), BF16),
            VMEM((RS, 2 * CAP), F32),
            VMEM((RG, 2 * CAP), F32),
            VMEM((RF, 2 * CAP), F32),
            VMEM((RF, 2 * CAP), F32),
            VMEM((RA, 2 * CAP), F32),
            pltpu.SemaphoreType.DMA((5,)),
        ],
        compiler_params=params(14),
        cost_estimate=COST,
        name="arrive_gy" if part else "arrive_gx",
    )(speeds, basis, grad, test, lift, *pieces, *outs)


def place_body(part, a, b, ad_in, ad_out, sems):
    copies = [
        pltpu.make_async_copy(src, ad_out.at[:, pl.ds(E + (part * 2 + q) * CAP, CAP)], sems.at[q])
        for q, src in enumerate((a, b))
    ]
    for c in copies:
        c.start()
    for c in copies:
        c.wait()


def place(part, pieces, ad_out):
    return pl.pallas_call(
        functools.partial(place_body, part),
        out_shape=jax.ShapeDtypeStruct((RA, 2 * E), F32),
        in_specs=[spec(), spec(), spec(ANY)],
        out_specs=spec(ANY),
        input_output_aliases={2: 0},
        scratch_shapes=[pltpu.SemaphoreType.DMA((2,))],
        compiler_params=params(4),
        cost_estimate=COST,
        name="place_gy" if part else "place_gx",
    )(*pieces, ad_out)


def after(value, done):
    return lax.optimization_barrier((value, done))


def exchange(axis, toward_high, toward_low):
    size = lax.axis_size(axis)
    up = [(i, i + 1) for i in range(size - 1)]
    down = [(j, i) for i, j in up]
    return lax.ppermute(toward_high, axis, up), lax.ppermute(toward_low, axis, down)


def per_device(
    state, adjoint, geometry, face_blocks, face_elem, move_ids, move_counts,
    basis, geo_grad, test_grad, lift, speeds,
):
    ids = move_ids
    owners = face_elem.reshape(2 * E // L, L)
    sgy = sg_first(ids, move_counts, state, geometry)
    sg_y = exchange("gy", *sgy)
    face_blocks, _ = after(face_blocks, sgy)
    fyu, fyd, fxu, fxd, keep, faces_out = faces_pack(ids, owners, move_counts, face_blocks)
    fp_y = exchange("gy", fyu, fyd)
    sxu, sxd, state_out, geometry_out = sg_second(ids, move_counts, keep, state, geometry)
    sg_x = exchange("gx", sxu, sxd)
    fp_x = exchange("gx", fxu, fxd)
    adjoint, _ = after(adjoint, (sxu, sxd))
    ayu, ayd, axu, axd, adjoint_out = adj_pack(ids, move_counts, keep, adjoint)
    ad_y = exchange("gy", ayu, ayd)
    ad_x = exchange("gx", axu, axd)
    weights = (speeds, basis.T, geo_grad.transpose(0, 2, 1), test_grad, lift.T)
    outs = arrive(0, weights, (*sg_x, *fp_x), (state_out, geometry_out, faces_out))
    adjoint_out = place(0, ad_x, adjoint_out)
    state_out, geometry_out, faces_out, residual = arrive(1, weights, (*sg_y, *fp_y), outs)
    adjoint_out = place(1, ad_y, adjoint_out)
    return state_out, adjoint_out, geometry_out, faces_out, residual


def solution(mesh):
    cols = P(None, ("gx", "gy"))
    flat = P(("gx", "gy"))
    return jax.shard_map(
        per_device,
        mesh=mesh,
        in_specs=(cols, cols, cols, cols, flat, P(("gx", "gy"), None), flat, P(), P(), P(), P(), P()),
        out_specs=(cols, cols, cols, cols, cols),
        check_vma=False,
    )
```

```python
import functools

import jax
import jax.numpy as jnp
from jax import lax
from jax.experimental import pallas as pl
from jax.experimental.pallas import tpu as pltpu
from jax.sharding import PartitionSpec as P

F32 = jnp.float32
BF16 = jnp.bfloat16
I32 = jnp.int32
VMEM = pltpu.VMEM
L = 128
NV, NS, NA, NQ, NFT = 5, 20, 35, 46, 15
QP = 48
E = 4096
CAP = 1024
RS, RA, RG, RF = NV * NS, NV * NA, 3 * NS, NV * NFT
RSG = RS + RG
RSGF = RSG + 2 * RF
VALS = NV * QP
WROWS = VALS + 9 * QP


def spec(space=pltpu.VMEM):
    return pl.BlockSpec(memory_space=space)


SMEM = pltpu.SMEM
HBM = pltpu.HBM
CHUNKS = 4


def params(mib):
    return pltpu.CompilerParams(vmem_limit_bytes=mib << 20)


SMALL = pl.CostEstimate(flops=1, transcendentals=0, bytes_accessed=1)
LARGE = pl.CostEstimate(flops=20_000_000_000, transcendentals=0, bytes_accessed=60_000_000)


def padded(block, rows):
    return jnp.concatenate([block, jnp.zeros((rows - block.shape[0], L), F32)], 0)


def at(c):
    return pl.ds(pl.multiple_of(c * L, L), L)


def copy_rows(ids, row, pairs):
    for j in range(L):
        e = ids[row, j]
        for src, dst in pairs:
            dst[pl.ds(j, 1), :] = src[pl.ds(e, 1), :]


def ids_to_scalar(cnt_h, cnt, ids_v, ids, sems, sides):
    copies = [pltpu.make_async_copy(cnt_h, cnt, sems.at[E // L])]
    for side in sides:
        for b in range(CAP // L):
            r = side * (CAP // L) + b
            copies.append(
                pltpu.make_async_copy(
                    ids_v.at[pl.ds(side, 1), pl.ds(b * L, L)], ids.at[pl.ds(r, 1), :], sems.at[r]
                )
            )
    for c in copies:
        c.start()
    return copies


def live_pairs(cnt, side):
    return (cnt[side] + 2 * L - 1) // (2 * L)


def fetch(pairs, sems):
    chunks = []
    for q in range(CHUNKS):
        group = []
        for m, (src, dst) in enumerate(pairs):
            width = src.shape[1] // CHUNKS
            cols = pl.ds(q * width, width)
            group.append(pltpu.make_async_copy(src.at[:, cols], dst.at[:, cols], sems.at[q, m]))
            group[-1].start()
        chunks.append(group)
    return chunks


def over_chunks(chunks, steps, body, unroll, carry=0):
    for q, group in enumerate(chunks):
        for c in group:
            c.wait()
        carry = lax.fori_loop(q * steps, (q + 1) * steps, body, carry, unroll=unroll)
    return carry


def live_lanes(cnt, side, block):
    return lax.broadcasted_iota(I32, (1, L), 1) + block * L < cnt[side]


def ids_scratch():
    return [pltpu.SMEM((4,), I32), pltpu.SMEM((E // L, L), I32), pltpu.SemaphoreType.DMA((E // L + 1,))]


def dot_nt(a, b):
    return lax.dot_general(a, b, (((1,), (1,)), ((), ())), preferred_element_type=F32)


def dot_nn(a, b):
    return lax.dot_general(a, b, (((1,), (0,)), ((), ())), preferred_element_type=F32)


def pack_loop(cnt, sides, outs, plan, bufs):
    for out, side in zip(outs, sides):

        def two(i, carry, out=out, side=side):
            for h in range(2):
                block = i * 2 + h
                live = live_lanes(cnt, side, block)
                m = 0
                for numbers, base, fields in plan:
                    pairs = [(src, bufs[h][m + k]) for k, (src, _, _) in enumerate(fields)]
                    copy_rows(numbers, base + side * (CAP // L) + block, pairs)
                    m += len(fields)
                m = 0
                for _, _, fields in plan:
                    for _, start, rows in fields:
                        back = bufs[h][m][...].T[:rows]
                        out[start : start + rows, at(block)] = jnp.where(live, back, 0.0)
                        m += 1
            return carry

        def blank(block, carry, out=out):
            out[:, at(block)] = jnp.zeros((out.shape[0], L), F32)
            return carry

        pairs_live = live_pairs(cnt, side)
        lax.fori_loop(0, pairs_live, two, 0)
        lax.fori_loop(pairs_live * 2, CAP // L, blank, 0)


def record_plan(ids, nums, xs, xg, xf):
    return (
        (ids, 0, [(xs, 0, RS), (xg, RS, RG)]),
        (nums, 0, [(xf, RSG, RF)]),
        (nums, E // L, [(xf, RSG + RF, RF)]),
    )


def buffers(refs):
    half = len(refs) // 2
    return refs[:half], refs[half:]


def onehots(row):
    hi32 = lax.broadcasted_iota(I32, (32, L), 0)
    lo128 = lax.broadcasted_iota(I32, (L, L), 0)
    return hi32 == (row >> 7), (lo128 == (row & 127)).astype(F32).astype(BF16)


def first_body(
    ids_h, owners_h, cnt_h, st_h, ge_h, fb_h, yu, yd, xs, xg, xf, nums, keep,
    ids_v, owners, st, ge, fb, nums_s, *rest,
):
    bufs, (sems, insem, fbsem, cnt, ids, idsem) = buffers(rest[:8]), rest[8:]
    own_copy = pltpu.make_async_copy(owners_h, owners, sems.at[0])
    own_copy.start()
    ids_copy = pltpu.make_async_copy(ids_h, ids_v, sems.at[1])
    ids_copy.start()
    moved = ids_to_scalar(cnt_h, cnt, ids_h, ids, idsem, (2, 3))
    chunks = fetch(((st_h, st), (ge_h, ge)), insem)
    face_chunks = fetch(((fb_h, fb),), fbsem)
    lane = lax.broadcasted_iota(I32, (1, L), 1)
    sq = lane * lane
    weights = [w.astype(F32) for w in (lane, sq >> 7, sq & 127)]
    nf = 2 * E // L
    ne = E // L
    unroll = 8
    own_copy.wait()
    ids_copy.wait()
    for c in moved:
        c.wait()

    def face_sums(g, carry):
        s1, s2 = carry
        for u in range(unroll):
            i = g * unroll + u
            mine, low = onehots(owners[pl.ds(i, 1), :])
            ones = mine.astype(F32)
            left = jnp.concatenate([ones] + [ones * w for w in weights], 0).astype(BF16)
            r = dot_nt(left, low).astype(I32)
            n, l, q = r[0:32], r[32:64], r[64:96] * 128 + r[96:128]
            base = i * L
            s1 = s1 + base * n + l
            s2 = s2 + base * base * n + 2 * base * l + q
            xf[at(i), :] = padded(fb[:, at(i)], L).T
            if u % 2 == 0:
                e = g * (unroll // 2) + u // 2
                xs[at(e), :] = padded(st[:, at(e)], L).T
                xg[at(e), :] = padded(ge[:, at(e)], L).T
        return s1, s2

    zero = jnp.zeros((32, L), I32)
    both = [p + q for p, q in zip(chunks, face_chunks)]
    s1, s2 = over_chunks(both, nf // unroll // CHUNKS, face_sums, 1, (zero, zero))
    gap = jnp.floor(jnp.sqrt((2 * s2 - s1 * s1).astype(F32)) + 0.5).astype(I32)
    first, second = (s1 - gap) >> 1, (s1 + gap) >> 1
    table = jnp.concatenate([first >> 7, first & 127, second >> 7, second & 127], 0)
    table = table.astype(F32).astype(BF16)
    dep = jnp.zeros((32, L), F32)
    to_scalar = []
    for side in (3, 2, 1, 0):
        for b in range(CAP // L):
            r = side * (CAP // L) + b
            mine, low = onehots(ids_v[side : side + 1, b * L : (b + 1) * L])
            live = (lane + b * L < cnt[side]).astype(F32)
            dep = dep + dot_nt((mine.astype(F32) * live).astype(BF16), low)
            found = dot_nn(table, low)
            pick = [
                jnp.sum(jnp.where(mine, found[32 * m : 32 * m + 32], 0.0), 0, keepdims=True)
                for m in range(4)
            ]
            nums[r : r + 1, :] = (pick[0] * 128.0 + pick[1]).astype(I32)
            nums[ne + r : ne + r + 1, :] = (pick[2] * 128.0 + pick[3]).astype(I32)
    to_scalar = pltpu.make_async_copy(nums, nums_s, sems.at[2])
    to_scalar.start()
    keep[...] = 1.0 - jnp.minimum(dep, 1.0)

    to_scalar.wait()
    pack_loop(cnt, (3, 2), (yu, yd), record_plan(ids, nums_s, xs, xg, xf), bufs)


def pack_first(ids, owners, cnt, st, ge, fb):
    return pl.pallas_call(
        first_body,
        out_shape=[jax.ShapeDtypeStruct((RSGF, CAP), F32)] * 2
        + [jax.ShapeDtypeStruct((E, L), F32)] * 2
        + [
            jax.ShapeDtypeStruct((2 * E, L), F32),
            jax.ShapeDtypeStruct((64, L), I32),
            jax.ShapeDtypeStruct((32, L), F32),
        ],
        in_specs=[spec(HBM)] * 6,
        out_specs=[spec()] * 7,
        scratch_shapes=[
            VMEM((4, CAP), I32),
            VMEM((64, L), I32),
            VMEM((RS, E), F32),
            VMEM((RG, E), F32),
            VMEM((RF, 2 * E), F32),
            SMEM((64, L), I32),
        ]
        + [VMEM((L, L), F32)] * 8
        + [
            pltpu.SemaphoreType.DMA((3,)),
            pltpu.SemaphoreType.DMA((CHUNKS, 2)),
            pltpu.SemaphoreType.DMA((CHUNKS, 1)),
        ]
        + ids_scratch(),
        compiler_params=params(20),
        cost_estimate=LARGE,
        name="pack_gy",
    )(*in_hbm(ids, owners, cnt, st, ge, fb))


def second_body(
    ids_h, owners_h, cnt_h, st_h, ge_h, fb_h, xs, xg, xf, nums, keep, xu, xd, st_out, ge_out, fb_out,
    owners, st, ge, fb, nums_s, *rest,
):
    bufs, (sems, insem, fbsem, cnt, ids, idsem) = buffers(rest[:8]), rest[8:]
    own_copy = pltpu.make_async_copy(owners_h, owners, sems.at[0])
    own_copy.start()
    to_scalar = pltpu.make_async_copy(nums, nums_s, sems.at[1])
    to_scalar.start()
    moved = ids_to_scalar(cnt_h, cnt, ids_h, ids, idsem, (0, 1))
    chunks = fetch(((st_h, st), (ge_h, ge)), insem)
    face_chunks = fetch(((fb_h, fb),), fbsem)
    for c in moved:
        c.wait()
    own_copy.wait()
    kept16 = keep[...].astype(BF16)

    def keep_faces(g, carry):
        for u in range(8):
            c = g * 8 + u
            mine, low = onehots(owners[pl.ds(c, 1), :])
            k = jnp.sum(jnp.where(mine, dot_nn(kept16, low), 0.0), 0, keepdims=True)
            fb[:, at(c)] = fb[:, at(c)] * k
        return carry

    def keep_elems(c, carry):
        k = keep[pl.ds(c, 1), :]
        st[:, at(c)] = st[:, at(c)] * k
        ge[:, at(c)] = ge[:, at(c)] * k
        return carry

    over_chunks(face_chunks, 2 * E // L // 8 // CHUNKS, keep_faces, 1)
    c0 = pltpu.make_async_copy(fb, fb_out.at[:, pl.ds(0, 2 * E)], sems.at[2])
    c0.start()
    over_chunks(chunks, E // L // CHUNKS, keep_elems, 2)
    c1 = pltpu.make_async_copy(st, st_out.at[:, pl.ds(0, E)], sems.at[3])
    c1.start()
    c2 = pltpu.make_async_copy(ge, ge_out.at[:, pl.ds(0, E)], sems.at[4])
    c2.start()
    to_scalar.wait()
    pack_loop(cnt, (1, 0), (xu, xd), record_plan(ids, nums_s, xs, xg, xf), bufs)
    for c in (c0, c1, c2):
        c.wait()


def pack_second(ids, owners, cnt, st, ge, fb, picked):
    return pl.pallas_call(
        second_body,
        out_shape=[jax.ShapeDtypeStruct((RSGF, CAP), F32)] * 2
        + [
            jax.ShapeDtypeStruct((RS, 2 * E), F32),
            jax.ShapeDtypeStruct((RG, 2 * E), F32),
            jax.ShapeDtypeStruct((RF, 4 * E), F32),
        ],
        in_specs=[spec(HBM)] * 6 + [spec()] * 5,
        out_specs=[spec(), spec(), spec(HBM), spec(HBM), spec(HBM)],
        scratch_shapes=[
            VMEM((64, L), I32),
            VMEM((RS, E), F32),
            VMEM((RG, E), F32),
            VMEM((RF, 2 * E), F32),
            SMEM((64, L), I32),
        ]
        + [VMEM((L, L), F32)] * 8
        + [
            pltpu.SemaphoreType.DMA((5,)),
            pltpu.SemaphoreType.DMA((CHUNKS, 2)),
            pltpu.SemaphoreType.DMA((CHUNKS, 1)),
        ]
        + ids_scratch(),
        compiler_params=params(20),
        cost_estimate=LARGE,
        name="pack_gx",
    )(*in_hbm(ids, owners, cnt, st, ge, fb), *picked)


def adj_body(
    ids_h, cnt_h, keep, ad_h, yu, yd, xu, xd, ad_out,
    ad, x0, x1, ka, a0, a1, b0, b1, sem, insem, cnt, ids, idsem,
):
    chunks = fetch(((ad_h, ad),), insem)
    moved = ids_to_scalar(cnt_h, cnt, ids_h, ids, idsem, range(4))

    def fwd(c, carry):
        k = keep[pl.ds(c, 1), :]
        p, q = ad[0:L, at(c)], ad[L:RA, at(c)]
        ka[0:L, at(c)] = p * k
        ka[L:RA, at(c)] = q * k
        x0[at(c), :] = p.T
        x1[at(c), :] = padded(q, L).T
        return carry

    over_chunks(chunks, E // L // CHUNKS, fwd, 2)
    c0 = pltpu.make_async_copy(ka, ad_out.at[:, pl.ds(0, E)], sem.at[0])
    c0.start()
    for c in moved:
        c.wait()
    plan = ((ids, 0, [(x0, 0, L), (x1, L, RA - L)]),)
    pack_loop(cnt, (3, 2, 1, 0), (yu, yd, xu, xd), plan, ((a0, a1), (b0, b1)))
    c0.wait()


def adj_pack(ids, cnt, keep, ad):
    return pl.pallas_call(
        adj_body,
        out_shape=[jax.ShapeDtypeStruct((RA, CAP), F32)] * 4
        + [jax.ShapeDtypeStruct((RA, 2 * E), F32)],
        in_specs=[spec(HBM), spec(HBM), spec(), spec(HBM)],
        out_specs=[spec()] * 4 + [spec(HBM)],
        scratch_shapes=[VMEM((RA, E), F32)]
        + [VMEM((E, L), F32)] * 2
        + [VMEM((RA, E), F32)]
        + [VMEM((L, L), F32)] * 4
        + [pltpu.SemaphoreType.DMA((1,)), pltpu.SemaphoreType.DMA((CHUNKS, 1))]
        + ids_scratch(),
        compiler_params=params(18),
        cost_estimate=LARGE,
        name="pack_adj",
    )(*in_hbm(ids, cnt), keep, *in_hbm(ad))


NB = 256


def split(x):
    hi = x.astype(BF16)
    return hi, (x - hi.astype(F32)).astype(BF16)


def arrive_body(
    part, first_call, speeds, basis, grad, test, lift, *rest,
):
    (xa, xb), rest = rest[:2], rest[2:]
    sg_a, sg_b = xa.at[pl.ds(0, RSG), :], xb.at[pl.ds(0, RSG), :]
    fp_a, fp_b = (x.at[pl.ds(RSG, 2 * RF), :] for x in (xa, xb))
    if first_call:
        st_in, ge_in, fb_in, st_out, ge_out, fb_out, res_out = rest[:7]
        rest = rest[7:]
    else:
        st_in, ge_in, fb_in, res_in, st_out, ge_out, fb_out, res_out = rest[:8]
        rest = rest[8:]
    wf, w3, tt, lf, ll, vj0, vj1, fh0, fh1, ks, kg, k1, k2, kr, sems = rest
    cols = pl.ds(E + part * 2 * CAP, 2 * CAP)

    wf[...] = jnp.zeros_like(wf)
    for v in range(NV):
        wf[v * NS : (v + 1) * NS, v * QP : v * QP + NQ] = basis[...]
    for c in range(3):
        for k in range(3):
            r = VALS + (c * 3 + k) * QP
            wf[RS + c * NS : RS + (c + 1) * NS, r : r + NQ] = grad[k]
    for r in range(0, 768, L):
        top = wf[0:L, r : r + L].T
        low = wf[L : 2 * L, r : r + L].T
        wide = jnp.concatenate([top, low], 1)[: min(L, WROWS - r)]
        wh, wl = split(wide[:, 0:RSG])
        here = slice(r, min(r + L, WROWS))
        w3[here, 0:RSG] = wh
        w3[here, RSG : 2 * RSG] = wh
        w3[here, 2 * RSG : 3 * RSG] = wl
    lf[...] = jnp.zeros_like(lf)
    lf[0:NA, 0 : 3 * QP] = jnp.zeros((NA, 3 * QP), F32)
    for k in range(3):
        lf[0:NA, k * QP : k * QP + NQ] = test[:, k * NQ : (k + 1) * NQ]
    th, tl = split(lf[0:48, 0 : 3 * QP])
    tt[0:48, :] = th
    tt[48:96, :] = tl
    lf[...] = jnp.zeros_like(lf)
    for v in range(NV):
        lf[v * NFT : (v + 1) * NFT, v * 40 : v * 40 + NA] = lift[...]
    lt = jnp.concatenate([lf[0:L, 0:L].T, lf[0:L, L : 2 * L].T], 0)
    lh, l2 = split(lt[0:208, 0:80])
    ll[0:208, :] = lh
    ll[208:416, :] = l2

    def block(b, sg, fp, d, vj, fh):
        src = slice(b * NB, (b + 1) * NB)
        dst = slice(d * CAP + b * NB, d * CAP + (b + 1) * NB)
        x = sg[:, src]
        ks[:, dst] = x[0:RS]
        kg[:, dst] = x[RS:RSG]
        f1, f2 = fp[0:RF, src], fp[RF : 2 * RF, src]
        k1[:, dst] = f1
        k2[:, dst] = f2
        hi, lo = split(x)
        vj[...] = dot_nn(w3[...], jnp.concatenate([hi, lo, hi], 0))
        for t in range(QP // 16):
            for h in range(NB // L):
                lanes = slice(h * L, (h + 1) * L)

                def part_of(r):
                    return vj[r + 16 * t : r + 16 * t + 16, lanes]

                jac = [[part_of(VALS + (c * 3 + k) * QP) for k in range(3)] for c in range(3)]
                flux = []
                for v in range(NV):
                    u = part_of(v * QP)
                    flux.append(u + u * (0.5 * jnp.tanh(u)))
                for k in range(3):
                    k1_, k2_ = (k + 1) % 3, (k + 2) % 3
                    cof = []
                    for c in range(3):
                        c1, c2 = (c + 1) % 3, (c + 2) % 3
                        cof.append(jac[c1][k1_] * jac[c2][k2_] - jac[c1][k2_] * jac[c2][k1_])
                    for v in range(NV):
                        w = cof[0] * speeds[0, v] + cof[1] * speeds[1, v] + cof[2] * speeds[2, v]
                        fhi, flo = split(w * flux[v])
                        r = k * QP + 16 * t
                        wide = slice(v * NB + h * L, v * NB + (h + 1) * L)
                        fh[0, r : r + 16, wide] = fhi
                        fh[1, r : r + 16, wide] = flo
        fs = jnp.concatenate([f1 + f2, jnp.zeros((80 - RF, NB), F32)], 0)
        shi, slo = split(fs)
        m1 = dot_nn(ll[...], shi)
        lifted = m1[0:208] + m1[208:416] + dot_nn(ll[0:208, :], slo)
        d1 = dot_nn(tt[...], fh[0])
        d2 = dot_nn(tt[0:48, :], fh[1])
        volume = d1[0:40] + d1[48:88] + d2[0:40]
        for v in range(NV):
            total = volume[:, v * NB : (v + 1) * NB] + lifted[40 * v : 40 * v + 40]
            kr[NA * v : NA * (v + 1), dst] = total[0:NA]

    for d, (sg, fp) in enumerate(((sg_a, fp_a), (sg_b, fp_b))):
        for b in range(CAP // NB):
            block(b, sg, fp, d, *((vj0, fh0), (vj1, fh1))[b % 2])
    copies = (
        (ks, st_out.at[:, cols]),
        (kg, ge_out.at[:, cols]),
        (k1, fb_out.at[:, pl.ds(2 * E + part * 2 * CAP, 2 * CAP)]),
        (k2, fb_out.at[:, pl.ds(3 * E + part * 2 * CAP, 2 * CAP)]),
        (kr, res_out.at[:, pl.ds(part * 2 * CAP, 2 * CAP)]),
    )
    copies = [pltpu.make_async_copy(s, t, sems.at[m]) for m, (s, t) in enumerate(copies)]
    for c in copies:
        c.start()
    for c in copies:
        c.wait()


def arrive(part, weights, pieces, outs):
    speeds, basis, grad, test, lift = weights
    first_call = len(outs) == 3
    shapes = [
        jax.ShapeDtypeStruct((RS, 2 * E), F32),
        jax.ShapeDtypeStruct((RG, 2 * E), F32),
        jax.ShapeDtypeStruct((RF, 4 * E), F32),
        jax.ShapeDtypeStruct((RA, E), F32),
    ]
    return pl.pallas_call(
        functools.partial(arrive_body, part, first_call),
        out_shape=shapes,
        in_specs=[spec(SMEM)] + [spec()] * (4 + len(pieces)) + [spec(HBM)] * len(outs),
        out_specs=[spec(HBM)] * 4,
        input_output_aliases={5 + len(pieces) + i: i for i in range(len(outs))},
        scratch_shapes=[
            VMEM((256, 768), F32),
            VMEM((WROWS, 3 * RSG), BF16),
            VMEM((96, 3 * QP), BF16),
            VMEM((208, 256), F32),
            VMEM((416, 80), BF16),
            VMEM((WROWS, NB), F32),
            VMEM((WROWS, NB), F32),
            VMEM((2, 3 * QP, NV * NB), BF16),
            VMEM((2, 3 * QP, NV * NB), BF16),
            VMEM((RS, 2 * CAP), F32),
            VMEM((RG, 2 * CAP), F32),
            VMEM((RF, 2 * CAP), F32),
            VMEM((RF, 2 * CAP), F32),
            VMEM((RA, 2 * CAP), F32),
            pltpu.SemaphoreType.DMA((5,)),
        ],
        compiler_params=params(22),
        cost_estimate=SMALL if part else LARGE,
        name="arrive_gy" if part else "arrive_gx",
    )(speeds, basis, grad, test, lift, *pieces, *outs)


def place_body(part, a, b, ad_in, ad_out, sems):
    copies = [
        pltpu.make_async_copy(src, ad_out.at[:, pl.ds(E + (part * 2 + q) * CAP, CAP)], sems.at[q])
        for q, src in enumerate((a, b))
    ]
    for c in copies:
        c.start()
    for c in copies:
        c.wait()


def place(part, pieces, ad_out):
    return pl.pallas_call(
        functools.partial(place_body, part),
        out_shape=jax.ShapeDtypeStruct((RA, 2 * E), F32),
        in_specs=[spec(), spec(), spec(HBM)],
        out_specs=spec(HBM),
        input_output_aliases={2: 0},
        scratch_shapes=[pltpu.SemaphoreType.DMA((2,))],
        compiler_params=params(4),
        cost_estimate=SMALL,
        name="place_gy" if part else "place_gx",
    )(*pieces, ad_out)


def in_hbm(*arrays):
    return [pltpu.with_memory_space_constraint(a, HBM) for a in arrays]


def after(value, done):
    return lax.optimization_barrier((value, done))


def exchange(axis, toward_high, toward_low):
    size = lax.axis_size(axis)
    up = [(i, i + 1) for i in range(size - 1)]
    down = [(j, i) for i, j in up]
    return lax.ppermute(toward_high, axis, up), lax.ppermute(toward_low, axis, down)


def per_device(
    state, adjoint, geometry, face_blocks, face_elem, move_ids, move_counts,
    basis, geo_grad, test_grad, lift, speeds,
):
    ids = move_ids
    owners = face_elem.reshape(2 * E // L, L)
    fields = (ids, owners, move_counts, state, geometry, face_blocks)
    yu, yd, *picked = pack_first(*fields)
    xu, xd, state_out, geometry_out, faces_out = pack_second(*fields, picked)
    in_x = exchange("gx", xu, xd)
    in_y = exchange("gy", yu, yd)
    keep = picked[-1]
    adjoint, _ = after(adjoint, (xu, xd))
    ayu, ayd, axu, axd, adjoint_out = adj_pack(ids, move_counts, keep, adjoint)
    (ayu, ayd), in_x = after((ayu, ayd), in_x)
    ad_y = exchange("gy", ayu, ayd)
    weights = (speeds, basis.T, geo_grad.transpose(0, 2, 1), test_grad, lift.T)
    outs = arrive(0, weights, in_x, (state_out, geometry_out, faces_out))
    (axu, axd, in_y), _ = after((axu, axd, in_y), outs[3])
    ad_x = exchange("gx", axu, axd)
    state_out, geometry_out, faces_out, residual = arrive(1, weights, in_y, outs)
    ad_y, _ = after(ad_y, residual)
    adjoint_out = place(1, ad_y, adjoint_out)
    adjoint_out = place(0, ad_x, adjoint_out)
    return state_out, adjoint_out, geometry_out, faces_out, residual


def solution(mesh):
    cols = P(None, ("gx", "gy"))
    flat = P(("gx", "gy"))
    return jax.shard_map(
        per_device,
        mesh=mesh,
        in_specs=(cols, cols, cols, cols, flat, P(("gx", "gy"), None), flat, P(), P(), P(), P(), P()),
        out_specs=(cols, cols, cols, cols, cols),
        check_vma=False,
    )
```

```python
import functools

import jax
import jax.numpy as jnp
from jax import lax
from jax.experimental import pallas as pl
from jax.experimental.pallas import tpu as pltpu
from jax.sharding import PartitionSpec as P

F32 = jnp.float32
BF16 = jnp.bfloat16
I32 = jnp.int32
VMEM = pltpu.VMEM
L = 128
NV, NS, NA, NQ, NFT = 5, 20, 35, 46, 15
QP = 48
E = 4096
CAP = 1024
RS, RA, RG, RF = NV * NS, NV * NA, 3 * NS, NV * NFT
RSG = RS + RG
RSGF = RSG + 2 * RF
ADJ0 = -(-RSGF // 8) * 8
RALL = ADJ0 + RA
VALS = NV * QP
WROWS = VALS + 9 * QP


def spec(space=pltpu.VMEM):
    return pl.BlockSpec(memory_space=space)


SMEM = pltpu.SMEM
HBM = pltpu.HBM
CHUNKS = 4


def params(mib):
    return pltpu.CompilerParams(vmem_limit_bytes=mib << 20)


SMALL = pl.CostEstimate(flops=1, transcendentals=0, bytes_accessed=1)
LARGE = pl.CostEstimate(flops=20_000_000_000, transcendentals=0, bytes_accessed=60_000_000)


def padded(block, rows):
    return jnp.concatenate([block, jnp.zeros((rows - block.shape[0], L), F32)], 0)


def at(c):
    return pl.ds(pl.multiple_of(c * L, L), L)


def copy_rows(ids, row, pairs):
    for j in range(L):
        e = ids[row, j]
        for src, dst in pairs:
            dst[pl.ds(j, 1), :] = src[pl.ds(e, 1), :]


def ids_to_scalar(cnt_h, cnt, ids_v, ids, sems, sides):
    copies = [pltpu.make_async_copy(cnt_h, cnt, sems.at[E // L])]
    for side in sides:
        for b in range(CAP // L):
            r = side * (CAP // L) + b
            copies.append(
                pltpu.make_async_copy(
                    ids_v.at[pl.ds(side, 1), pl.ds(b * L, L)], ids.at[pl.ds(r, 1), :], sems.at[r]
                )
            )
    for c in copies:
        c.start()
    return copies


def live_pairs(cnt, side):
    return (cnt[side] + 2 * L - 1) // (2 * L)


def fetch(pairs, sems):
    chunks = []
    for q in range(CHUNKS):
        group = []
        for m, (src, dst) in enumerate(pairs):
            width = src.shape[1] // CHUNKS
            cols = pl.ds(q * width, width)
            group.append(pltpu.make_async_copy(src.at[:, cols], dst.at[:, cols], sems.at[q, m]))
            group[-1].start()
        chunks.append(group)
    return chunks


def over_chunks(chunks, steps, body, unroll, carry=0):
    for q, group in enumerate(chunks):
        for c in group:
            c.wait()
        carry = lax.fori_loop(q * steps, (q + 1) * steps, body, carry, unroll=unroll)
    return carry


def live_lanes(cnt, side, block):
    return lax.broadcasted_iota(I32, (1, L), 1) + block * L < cnt[side]


def ids_scratch():
    return [pltpu.SMEM((4,), I32), pltpu.SMEM((E // L, L), I32), pltpu.SemaphoreType.DMA((E // L + 1,))]


def dot_nt(a, b):
    return lax.dot_general(a, b, (((1,), (1,)), ((), ())), preferred_element_type=F32)


def dot_nn(a, b):
    return lax.dot_general(a, b, (((1,), (0,)), ((), ())), preferred_element_type=F32)


def pack_loop(cnt, sides, outs, plan, bufs):
    for out, side in zip(outs, sides):

        def two(i, carry, out=out, side=side):
            for h in range(2):
                block = i * 2 + h
                live = live_lanes(cnt, side, block)
                m = 0
                for numbers, base, fields in plan:
                    pairs = [(src, bufs[h][m + k]) for k, (src, _, _) in enumerate(fields)]
                    copy_rows(numbers, base + side * (CAP // L) + block, pairs)
                    m += len(fields)
                m = 0
                for _, _, fields in plan:
                    for _, start, rows in fields:
                        back = bufs[h][m][...].T[:rows]
                        out[start : start + rows, at(block)] = jnp.where(live, back, 0.0)
                        m += 1
            return carry

        def blank(block, carry, out=out):
            out[:, at(block)] = jnp.zeros((out.shape[0], L), F32)
            return carry

        pairs_live = live_pairs(cnt, side)
        lax.fori_loop(0, pairs_live, two, 0)
        lax.fori_loop(pairs_live * 2, CAP // L, blank, 0)


def record_plan(ids, nums, xs, xg, xf):
    return (
        (ids, 0, [(xs, 0, RS), (xg, RS, RG)]),
        (nums, 0, [(xf, RSG, RF)]),
        (nums, E // L, [(xf, RSG + RF, RF)]),
    )


def buffers(refs):
    half = len(refs) // 2
    return refs[:half], refs[half:]


def onehots(row):
    hi32 = lax.broadcasted_iota(I32, (32, L), 0)
    lo128 = lax.broadcasted_iota(I32, (L, L), 0)
    return hi32 == (row >> 7), (lo128 == (row & 127)).astype(F32).astype(BF16)


def first_body(
    ids_h, owners_h, cnt_h, st_h, ge_h, fb_h, yu, yd, xs, xg, xf, nums, keep,
    ids_v, owners, st, ge, fb, nums_s, *rest,
):
    bufs, (sems, insem, fbsem, cnt, ids, idsem) = buffers(rest[:8]), rest[8:]
    own_copy = pltpu.make_async_copy(owners_h, owners, sems.at[0])
    own_copy.start()
    ids_copy = pltpu.make_async_copy(ids_h, ids_v, sems.at[1])
    ids_copy.start()
    moved = ids_to_scalar(cnt_h, cnt, ids_h, ids, idsem, (2, 3))
    chunks = fetch(((st_h, st), (ge_h, ge)), insem)
    face_chunks = fetch(((fb_h, fb),), fbsem)
    lane = lax.broadcasted_iota(I32, (1, L), 1)
    sq = lane * lane
    weights = [w.astype(F32) for w in (lane, sq >> 7, sq & 127)]
    nf = 2 * E // L
    ne = E // L
    unroll = 8
    own_copy.wait()
    ids_copy.wait()
    for c in moved:
        c.wait()

    def face_sums(g, carry):
        s1, s2 = carry
        for u in range(unroll):
            i = g * unroll + u
            mine, low = onehots(owners[pl.ds(i, 1), :])
            ones = mine.astype(F32)
            left = jnp.concatenate([ones] + [ones * w for w in weights], 0).astype(BF16)
            r = dot_nt(left, low).astype(I32)
            n, l, q = r[0:32], r[32:64], r[64:96] * 128 + r[96:128]
            base = i * L
            s1 = s1 + base * n + l
            s2 = s2 + base * base * n + 2 * base * l + q
            xf[at(i), :] = padded(fb[:, at(i)], L).T
            if u % 2 == 0:
                e = g * (unroll // 2) + u // 2
                xs[at(e), :] = padded(st[:, at(e)], L).T
                xg[at(e), :] = padded(ge[:, at(e)], L).T
        return s1, s2

    zero = jnp.zeros((32, L), I32)
    both = [p + q for p, q in zip(chunks, face_chunks)]
    s1, s2 = over_chunks(both, nf // unroll // CHUNKS, face_sums, 1, (zero, zero))
    gap = jnp.floor(jnp.sqrt((2 * s2 - s1 * s1).astype(F32)) + 0.5).astype(I32)
    first, second = (s1 - gap) >> 1, (s1 + gap) >> 1
    table = jnp.concatenate([first >> 7, first & 127, second >> 7, second & 127], 0)
    table = table.astype(F32).astype(BF16)
    dep = jnp.zeros((32, L), F32)
    to_scalar = []
    for side in (3, 2, 1, 0):
        for b in range(CAP // L):
            r = side * (CAP // L) + b
            mine, low = onehots(ids_v[side : side + 1, b * L : (b + 1) * L])
            live = (lane + b * L < cnt[side]).astype(F32)
            dep = dep + dot_nt((mine.astype(F32) * live).astype(BF16), low)
            found = dot_nn(table, low)
            pick = [
                jnp.sum(jnp.where(mine, found[32 * m : 32 * m + 32], 0.0), 0, keepdims=True)
                for m in range(4)
            ]
            nums[r : r + 1, :] = (pick[0] * 128.0 + pick[1]).astype(I32)
            nums[ne + r : ne + r + 1, :] = (pick[2] * 128.0 + pick[3]).astype(I32)
    to_scalar = pltpu.make_async_copy(nums, nums_s, sems.at[2])
    to_scalar.start()
    keep[...] = 1.0 - jnp.minimum(dep, 1.0)

    to_scalar.wait()
    pack_loop(cnt, (3, 2), (yu, yd), record_plan(ids, nums_s, xs, xg, xf), bufs)


def pack_first(ids, owners, cnt, st, ge, fb):
    return pl.pallas_call(
        first_body,
        out_shape=[jax.ShapeDtypeStruct((RSGF, CAP), F32)] * 2
        + [jax.ShapeDtypeStruct((E, L), F32)] * 2
        + [
            jax.ShapeDtypeStruct((2 * E, L), F32),
            jax.ShapeDtypeStruct((64, L), I32),
            jax.ShapeDtypeStruct((32, L), F32),
        ],
        in_specs=[spec(HBM)] * 6,
        out_specs=[spec()] * 7,
        scratch_shapes=[
            VMEM((4, CAP), I32),
            VMEM((64, L), I32),
            VMEM((RS, E), F32),
            VMEM((RG, E), F32),
            VMEM((RF, 2 * E), F32),
            SMEM((64, L), I32),
        ]
        + [VMEM((L, L), F32)] * 8
        + [
            pltpu.SemaphoreType.DMA((3,)),
            pltpu.SemaphoreType.DMA((CHUNKS, 2)),
            pltpu.SemaphoreType.DMA((CHUNKS, 1)),
        ]
        + ids_scratch(),
        compiler_params=params(20),
        cost_estimate=LARGE,
        name="pack_gy",
    )(*in_hbm(ids, owners, cnt, st, ge, fb))


def rest_body(
    ids_h, cnt_h, ad_h, xs, xg, xf, nums, xu, xd, yu, yd, ad, x0, x1, nums_s, *rest,
):
    (insem, numsem, cnt, ids, idsem) = rest[12:]
    bufs = buffers(rest[:12])
    to_scalar = pltpu.make_async_copy(nums, nums_s, numsem)
    to_scalar.start()
    chunks = fetch(((ad_h, ad),), insem)
    moved = ids_to_scalar(cnt_h, cnt, ids_h, ids, idsem, range(4))

    def fwd(c, carry):
        x0[at(c), :] = ad[0:L, at(c)].T
        x1[at(c), :] = padded(ad[L:RA, at(c)], L).T
        return carry

    over_chunks(chunks, E // L // CHUNKS, fwd, 4)
    for c in moved:
        c.wait()
    to_scalar.wait()
    faces = record_plan(ids, nums_s, xs, xg, xf)
    elems = (ids, 0, [*faces[0][2], (x0, ADJ0, L), (x1, ADJ0 + L, RA - L)])
    pack_loop(cnt, (1, 0), (xu, xd), (elems, *faces[1:]), bufs)
    pack_loop(cnt, (3, 2), (yu, yd), ((ids, 0, [(x0, 0, L), (x1, L, RA - L)]),), bufs)


def pack_rest(ids, cnt, ad, picked):
    return pl.pallas_call(
        rest_body,
        out_shape=[jax.ShapeDtypeStruct((RALL, CAP), F32)] * 2
        + [jax.ShapeDtypeStruct((RA, CAP), F32)] * 2,
        in_specs=[spec(HBM)] * 3 + [spec()] * 4,
        out_specs=[spec()] * 4,
        scratch_shapes=[VMEM((RA, E), F32)]
        + [VMEM((E, L), F32)] * 2
        + [SMEM((64, L), I32)]
        + [VMEM((L, L), F32)] * 12
        + [pltpu.SemaphoreType.DMA((CHUNKS, 1)), pltpu.SemaphoreType.DMA]
        + ids_scratch(),
        compiler_params=params(22),
        cost_estimate=LARGE,
        name="pack_rest",
    )(*in_hbm(ids, cnt, ad), *picked)


def keep_body(
    owners_h, st_h, ad_h, ge_h, fb_h, keep, st_out, ad_out, ge_out, fb_out,
    owners, st, ad, ge, fb, insem, outsem, sem,
):
    own_copy = pltpu.make_async_copy(owners_h, owners, sem)
    own_copy.start()
    local = (st, ad, ge, fb)
    chunks = fetch(list(zip((st_h, ad_h, ge_h, fb_h), local)), insem)
    own_copy.wait()
    kept16 = keep[...].astype(BF16)
    back = []

    def scale(g, carry):
        for u in range(8):
            c = g * 8 + u
            mine, low = onehots(owners[pl.ds(c, 1), :])
            k = jnp.sum(jnp.where(mine, dot_nn(kept16, low), 0.0), 0, keepdims=True)
            fb[:, at(c)] = fb[:, at(c)] * k
        for u in range(4):
            c = g * 4 + u
            k = keep[pl.ds(c, 1), :]
            for x in (st, ad, ge):
                x[:, at(c)] = x[:, at(c)] * k
        return carry

    steps = E // L // 4 // CHUNKS
    for q, group in enumerate(chunks):
        for c in group:
            c.wait()
        lax.fori_loop(q * steps, (q + 1) * steps, scale, 0)
        for m, (x, out) in enumerate(zip(local, (st_out, ad_out, ge_out, fb_out))):
            width = x.shape[1] // CHUNKS
            cols = pl.ds(q * width, width)
            back.append(pltpu.make_async_copy(x.at[:, cols], out.at[:, cols], outsem.at[q, m]))
            back[-1].start()
    for c in back:
        c.wait()


def keep_own(owners, st, ad, ge, fb, keep):
    return pl.pallas_call(
        keep_body,
        out_shape=[
            jax.ShapeDtypeStruct((RS, 2 * E), F32),
            jax.ShapeDtypeStruct((RA, 2 * E), F32),
            jax.ShapeDtypeStruct((RG, 2 * E), F32),
            jax.ShapeDtypeStruct((RF, 4 * E), F32),
        ],
        in_specs=[spec(HBM)] * 5 + [spec()],
        out_specs=[spec(HBM)] * 4,
        scratch_shapes=[
            VMEM((64, L), I32),
            VMEM((RS, E), F32),
            VMEM((RA, E), F32),
            VMEM((RG, E), F32),
            VMEM((RF, 2 * E), F32),
            pltpu.SemaphoreType.DMA((CHUNKS, 4)),
            pltpu.SemaphoreType.DMA((CHUNKS, 4)),
            pltpu.SemaphoreType.DMA,
        ],
        compiler_params=params(12),
        cost_estimate=LARGE,
        name="keep_own",
    )(*in_hbm(owners, st, ad, ge, fb), keep)


NB = 256


def split(x):
    hi = x.astype(BF16)
    return hi, (x - hi.astype(F32)).astype(BF16)


def arrive_body(
    part, first_call, speeds, basis, grad, test, lift, *rest,
):
    (xa, xb), rest = rest[:2], rest[2:]
    if first_call:
        st_in, ge_in, fb_in, st_out, ge_out, fb_out, res_out = rest[:7]
        rest = rest[7:]
    else:
        st_in, ge_in, fb_in, res_in, ad_in, st_out, ge_out, fb_out, res_out, ad_out = rest[:10]
        rest = rest[10:]
    wf, w3, tt, lf, ll, vj0, vj1, fh0, fh1, ks, kg, k1, k2, kr, sems = rest
    cols = pl.ds(E + part * 2 * CAP, 2 * CAP)

    adj_copies = []
    if not first_call:
        for q, x in enumerate((xa, xb)):
            to = ad_out.at[:, pl.ds(E + (part * 2 + q) * CAP, CAP)]
            adj_copies.append(pltpu.make_async_copy(x.at[pl.ds(ADJ0, RA), :], to, sems.at[5 + q]))
            adj_copies[-1].start()
    wf[...] = jnp.zeros_like(wf)
    for v in range(NV):
        wf[v * NS : (v + 1) * NS, v * QP : v * QP + NQ] = basis[...]
    for c in range(3):
        for k in range(3):
            r = VALS + (c * 3 + k) * QP
            wf[RS + c * NS : RS + (c + 1) * NS, r : r + NQ] = grad[k]
    for r in range(0, 768, L):
        top = wf[0:L, r : r + L].T
        low = wf[L : 2 * L, r : r + L].T
        wide = jnp.concatenate([top, low], 1)[: min(L, WROWS - r)]
        wh, wl = split(wide[:, 0:RSG])
        here = slice(r, min(r + L, WROWS))
        w3[here, 0:RSG] = wh
        w3[here, RSG : 2 * RSG] = wh
        w3[here, 2 * RSG : 3 * RSG] = wl
    lf[...] = jnp.zeros_like(lf)
    lf[0:NA, 0 : 3 * QP] = jnp.zeros((NA, 3 * QP), F32)
    for k in range(3):
        lf[0:NA, k * QP : k * QP + NQ] = test[:, k * NQ : (k + 1) * NQ]
    th, tl = split(lf[0:48, 0 : 3 * QP])
    tt[0:48, :] = th
    tt[48:96, :] = tl
    lf[...] = jnp.zeros_like(lf)
    for v in range(NV):
        lf[v * NFT : (v + 1) * NFT, v * 40 : v * 40 + NA] = lift[...]
    lt = jnp.concatenate([lf[0:L, 0:L].T, lf[0:L, L : 2 * L].T], 0)
    lh, l2 = split(lt[0:208, 0:80])
    ll[0:208, :] = lh
    ll[208:416, :] = l2

    def block(b, rec, d, vj, fh):
        src = slice(b * NB, (b + 1) * NB)
        dst = slice(d * CAP + b * NB, d * CAP + (b + 1) * NB)
        x = rec[0:RSG, src]
        ks[:, dst] = x[0:RS]
        kg[:, dst] = x[RS:RSG]
        f1, f2 = rec[RSG : RSG + RF, src], rec[RSG + RF : RSGF, src]
        k1[:, dst] = f1
        k2[:, dst] = f2
        hi, lo = split(x)
        vj[...] = dot_nn(w3[...], jnp.concatenate([hi, lo, hi], 0))
        for t in range(QP // 16):
            for h in range(NB // L):
                lanes = slice(h * L, (h + 1) * L)

                def part_of(r):
                    return vj[r + 16 * t : r + 16 * t + 16, lanes]

                jac = [[part_of(VALS + (c * 3 + k) * QP) for k in range(3)] for c in range(3)]
                flux = []
                for v in range(NV):
                    u = part_of(v * QP)
                    flux.append(u + u * (0.5 * jnp.tanh(u)))
                for k in range(3):
                    k1_, k2_ = (k + 1) % 3, (k + 2) % 3
                    cof = []
                    for c in range(3):
                        c1, c2 = (c + 1) % 3, (c + 2) % 3
                        cof.append(jac[c1][k1_] * jac[c2][k2_] - jac[c1][k2_] * jac[c2][k1_])
                    for v in range(NV):
                        w = cof[0] * speeds[0, v] + cof[1] * speeds[1, v] + cof[2] * speeds[2, v]
                        fhi, flo = split(w * flux[v])
                        r = k * QP + 16 * t
                        wide = slice(v * NB + h * L, v * NB + (h + 1) * L)
                        fh[0, r : r + 16, wide] = fhi
                        fh[1, r : r + 16, wide] = flo
        fs = jnp.concatenate([f1 + f2, jnp.zeros((80 - RF, NB), F32)], 0)
        shi, slo = split(fs)
        m1 = dot_nn(ll[...], shi)
        lifted = m1[0:208] + m1[208:416] + dot_nn(ll[0:208, :], slo)
        d1 = dot_nn(tt[...], fh[0])
        d2 = dot_nn(tt[0:48, :], fh[1])
        volume = d1[0:40] + d1[48:88] + d2[0:40]
        for v in range(NV):
            total = volume[:, v * NB : (v + 1) * NB] + lifted[40 * v : 40 * v + 40]
            kr[NA * v : NA * (v + 1), dst] = total[0:NA]

    for d, rec in enumerate((xa, xb)):
        for b in range(CAP // NB):
            block(b, rec, d, *((vj0, fh0), (vj1, fh1))[b % 2])
    copies = (
        (ks, st_out.at[:, cols]),
        (kg, ge_out.at[:, cols]),
        (k1, fb_out.at[:, pl.ds(2 * E + part * 2 * CAP, 2 * CAP)]),
        (k2, fb_out.at[:, pl.ds(3 * E + part * 2 * CAP, 2 * CAP)]),
        (kr, res_out.at[:, pl.ds(part * 2 * CAP, 2 * CAP)]),
    )
    copies = [pltpu.make_async_copy(s, t, sems.at[m]) for m, (s, t) in enumerate(copies)]
    for c in copies:
        c.start()
    for c in copies + adj_copies:
        c.wait()


def arrive(part, weights, pieces, outs):
    speeds, basis, grad, test, lift = weights
    first_call = len(outs) == 3
    shapes = [
        jax.ShapeDtypeStruct((RS, 2 * E), F32),
        jax.ShapeDtypeStruct((RG, 2 * E), F32),
        jax.ShapeDtypeStruct((RF, 4 * E), F32),
        jax.ShapeDtypeStruct((RA, E), F32),
    ] + [jax.ShapeDtypeStruct((RA, 2 * E), F32)] * (len(outs) == 5)
    return pl.pallas_call(
        functools.partial(arrive_body, part, first_call),
        out_shape=shapes,
        in_specs=[spec(SMEM)] + [spec()] * (4 + len(pieces)) + [spec(HBM)] * len(outs),
        out_specs=[spec(HBM)] * len(shapes),
        input_output_aliases={5 + len(pieces) + i: i for i in range(len(outs))},
        scratch_shapes=[
            VMEM((256, 768), F32),
            VMEM((WROWS, 3 * RSG), BF16),
            VMEM((96, 3 * QP), BF16),
            VMEM((208, 256), F32),
            VMEM((416, 80), BF16),
            VMEM((WROWS, NB), F32),
            VMEM((WROWS, NB), F32),
            VMEM((2, 3 * QP, NV * NB), BF16),
            VMEM((2, 3 * QP, NV * NB), BF16),
            VMEM((RS, 2 * CAP), F32),
            VMEM((RG, 2 * CAP), F32),
            VMEM((RF, 2 * CAP), F32),
            VMEM((RF, 2 * CAP), F32),
            VMEM((RA, 2 * CAP), F32),
            pltpu.SemaphoreType.DMA((7,)),
        ],
        compiler_params=params(24),
        cost_estimate=SMALL if part else SMALL,
        name="arrive_gy" if part else "arrive_gx",
    )(speeds, basis, grad, test, lift, *pieces, *outs)


def place_body(part, a, b, ad_in, ad_out, sems):
    copies = [
        pltpu.make_async_copy(src, ad_out.at[:, pl.ds(E + (part * 2 + q) * CAP, CAP)], sems.at[q])
        for q, src in enumerate((a, b))
    ]
    for c in copies:
        c.start()
    for c in copies:
        c.wait()


def place(part, pieces, ad_out):
    return pl.pallas_call(
        functools.partial(place_body, part),
        out_shape=jax.ShapeDtypeStruct((RA, 2 * E), F32),
        in_specs=[spec(), spec(), spec(HBM)],
        out_specs=spec(HBM),
        input_output_aliases={2: 0},
        scratch_shapes=[pltpu.SemaphoreType.DMA((2,))],
        compiler_params=params(4),
        cost_estimate=SMALL,
        name="place_gy" if part else "place_gx",
    )(*pieces, ad_out)


def in_hbm(*arrays):
    return [pltpu.with_memory_space_constraint(a, HBM) for a in arrays]


def after(value, done):
    return lax.optimization_barrier((value, done))


def exchange(axis, toward_high, toward_low):
    size = lax.axis_size(axis)
    up = [(i, i + 1) for i in range(size - 1)]
    down = [(j, i) for i, j in up]
    return lax.ppermute(toward_high, axis, up), lax.ppermute(toward_low, axis, down)


def per_device(
    state, adjoint, geometry, face_blocks, face_elem, move_ids, move_counts,
    basis, geo_grad, test_grad, lift, speeds,
):
    ids = move_ids
    owners = face_elem.reshape(2 * E // L, L)
    yu, yd, *picked, keep = pack_first(ids, owners, move_counts, state, geometry, face_blocks)
    in_y = exchange("gy", yu, yd)
    xu, xd, ayu, ayd = pack_rest(ids, move_counts, adjoint, picked)
    in_x = exchange("gx", xu, xd)
    keep, _ = after(keep, (xu, xd))
    state_out, adjoint_out, geometry_out, faces_out = keep_own(
        owners, state, adjoint, geometry, face_blocks, keep
    )
    (ayu, ayd, in_y), _ = after((ayu, ayd, in_y), faces_out)
    ad_y = exchange("gy", ayu, ayd)
    weights = (speeds, basis.T, geo_grad.transpose(0, 2, 1), test_grad, lift.T)
    outs = arrive(1, weights, in_y, (state_out, geometry_out, faces_out))
    outs = arrive(0, weights, in_x, (*outs, adjoint_out))
    state_out, geometry_out, faces_out, residual, adjoint_out = outs
    ad_y, _ = after(ad_y, residual)
    adjoint_out = place(1, ad_y, adjoint_out)
    return state_out, adjoint_out, geometry_out, faces_out, residual


def solution(mesh):
    cols = P(None, ("gx", "gy"))
    flat = P(("gx", "gy"))
    return jax.shard_map(
        per_device,
        mesh=mesh,
        in_specs=(cols, cols, cols, cols, flat, P(("gx", "gy"), None), flat, P(), P(), P(), P(), P()),
        out_specs=(cols, cols, cols, cols, cols),
        check_vma=False,
    )
```

```python
import functools

import jax
import jax.numpy as jnp
from jax import lax
from jax.experimental import pallas as pl
from jax.experimental.pallas import tpu as pltpu
from jax.sharding import PartitionSpec as P

F32 = jnp.float32
BF16 = jnp.bfloat16
I32 = jnp.int32
VMEM = pltpu.VMEM
L = 128
NV, NS, NA, NQ, NFT = 5, 20, 35, 46, 15
QP = 48
E = 4096
CAP = 1024
RS, RA, RG, RF = NV * NS, NV * NA, 3 * NS, NV * NFT
RSG = RS + RG
RSGF = RSG + 2 * RF
ADJ0 = -(-RSGF // 8) * 8
RALL = ADJ0 + RA
VALS = NV * QP
WROWS = VALS + 9 * QP


def spec(space=pltpu.VMEM):
    return pl.BlockSpec(memory_space=space)


SMEM = pltpu.SMEM
HBM = pltpu.HBM
CHUNKS = 4
KEEP_PARTS = 8


def params(mib):
    return pltpu.CompilerParams(vmem_limit_bytes=mib << 20)


SMALL = pl.CostEstimate(flops=1, transcendentals=0, bytes_accessed=1)
LARGE = pl.CostEstimate(flops=20_000_000_000, transcendentals=0, bytes_accessed=60_000_000)


def padded(block, rows):
    return jnp.concatenate([block, jnp.zeros((rows - block.shape[0], L), F32)], 0)


def at(c):
    return pl.ds(pl.multiple_of(c * L, L), L)


def copy_rows(ids, row, pairs):
    for j in range(L):
        e = ids[row, j]
        for src, dst in pairs:
            dst[pl.ds(j, 1), :] = src[pl.ds(e, 1), :]


def ids_to_scalar(cnt_h, cnt, ids_v, ids, sems, sides):
    copies = [pltpu.make_async_copy(cnt_h, cnt, sems.at[E // L])]
    for side in sides:
        for b in range(CAP // L):
            r = side * (CAP // L) + b
            copies.append(
                pltpu.make_async_copy(
                    ids_v.at[pl.ds(side, 1), pl.ds(b * L, L)], ids.at[pl.ds(r, 1), :], sems.at[r]
                )
            )
    for c in copies:
        c.start()
    return copies


def live_pairs(cnt, side):
    return (cnt[side] + 2 * L - 1) // (2 * L)


def fetch(pairs, sems, parts=CHUNKS):
    chunks = []
    for q in range(parts):
        group = []
        for m, (src, dst) in enumerate(pairs):
            width = src.shape[1] // parts
            cols = pl.ds(q * width, width)
            group.append(pltpu.make_async_copy(src.at[:, cols], dst.at[:, cols], sems.at[q, m]))
            group[-1].start()
        chunks.append(group)
    return chunks


def over_chunks(chunks, steps, body, unroll, carry=0):
    for q, group in enumerate(chunks):
        for c in group:
            c.wait()
        carry = lax.fori_loop(q * steps, (q + 1) * steps, body, carry, unroll=unroll)
    return carry


def live_lanes(cnt, side, block):
    return lax.broadcasted_iota(I32, (1, L), 1) + block * L < cnt[side]


def ids_scratch():
    return [pltpu.SMEM((4,), I32), pltpu.SMEM((E // L, L), I32), pltpu.SemaphoreType.DMA((E // L + 1,))]


def dot_nt(a, b):
    return lax.dot_general(a, b, (((1,), (1,)), ((), ())), preferred_element_type=F32)


def dot_nn(a, b):
    return lax.dot_general(a, b, (((1,), (0,)), ((), ())), preferred_element_type=F32)


def pack_loop(cnt, sides, outs, plan, bufs):
    for out, side in zip(outs, sides):

        def two(i, carry, out=out, side=side):
            for h in range(2):
                block = i * 2 + h
                live = live_lanes(cnt, side, block)
                m = 0
                for numbers, base, fields in plan:
                    pairs = [(src, bufs[h][m + k]) for k, (src, _, _) in enumerate(fields)]
                    copy_rows(numbers, base + side * (CAP // L) + block, pairs)
                    m += len(fields)
                m = 0
                for _, _, fields in plan:
                    for _, start, rows in fields:
                        back = bufs[h][m][...].T[:rows]
                        out[start : start + rows, at(block)] = jnp.where(live, back, 0.0)
                        m += 1
            return carry

        def blank(block, carry, out=out):
            out[:, at(block)] = jnp.zeros((out.shape[0], L), F32)
            return carry

        pairs_live = live_pairs(cnt, side)
        lax.fori_loop(0, pairs_live, two, 0)
        lax.fori_loop(pairs_live * 2, CAP // L, blank, 0)


def record_plan(ids, nums, xs, xg, xf):
    return (
        (ids, 0, [(xs, 0, RS), (xg, RS, RG)]),
        (nums, 0, [(xf, RSG, RF)]),
        (nums, E // L, [(xf, RSG + RF, RF)]),
    )


def buffers(refs):
    half = len(refs) // 2
    return refs[:half], refs[half:]


def onehots(row):
    hi32 = lax.broadcasted_iota(I32, (32, L), 0)
    lo128 = lax.broadcasted_iota(I32, (L, L), 0)
    return hi32 == (row >> 7), (lo128 == (row & 127)).astype(F32).astype(BF16)


def first_body(
    ids_h, owners_h, cnt_h, st_h, ge_h, fb_h, yu, yd, xs, xg, xf, nums, keep,
    ids_v, owners, st, ge, fb, nums_s, *rest,
):
    bufs, (sems, insem, fbsem, cnt, ids, idsem) = buffers(rest[:8]), rest[8:]
    own_copy = pltpu.make_async_copy(owners_h, owners, sems.at[0])
    own_copy.start()
    ids_copy = pltpu.make_async_copy(ids_h, ids_v, sems.at[1])
    ids_copy.start()
    moved = ids_to_scalar(cnt_h, cnt, ids_h, ids, idsem, (2, 3))
    chunks = fetch(((st_h, st), (ge_h, ge)), insem)
    face_chunks = fetch(((fb_h, fb),), fbsem)
    lane = lax.broadcasted_iota(I32, (1, L), 1)
    sq = lane * lane
    weights = [w.astype(F32) for w in (lane, sq >> 7, sq & 127)]
    nf = 2 * E // L
    ne = E // L
    unroll = 8
    own_copy.wait()
    ids_copy.wait()
    for c in moved:
        c.wait()

    def face_sums(g, carry):
        s1, s2 = carry
        for u in range(unroll):
            i = g * unroll + u
            mine, low = onehots(owners[pl.ds(i, 1), :])
            ones = mine.astype(F32)
            left = jnp.concatenate([ones] + [ones * w for w in weights], 0).astype(BF16)
            r = dot_nt(left, low).astype(I32)
            n, l, q = r[0:32], r[32:64], r[64:96] * 128 + r[96:128]
            base = i * L
            s1 = s1 + base * n + l
            s2 = s2 + base * base * n + 2 * base * l + q
            xf[at(i), :] = padded(fb[:, at(i)], L).T
            if u % 2 == 0:
                e = g * (unroll // 2) + u // 2
                xs[at(e), :] = padded(st[:, at(e)], L).T
                xg[at(e), :] = padded(ge[:, at(e)], L).T
        return s1, s2

    zero = jnp.zeros((32, L), I32)
    both = [p + q for p, q in zip(chunks, face_chunks)]
    s1, s2 = over_chunks(both, nf // unroll // CHUNKS, face_sums, 1, (zero, zero))
    gap = jnp.floor(jnp.sqrt((2 * s2 - s1 * s1).astype(F32)) + 0.5).astype(I32)
    first, second = (s1 - gap) >> 1, (s1 + gap) >> 1
    table = jnp.concatenate([first >> 7, first & 127, second >> 7, second & 127], 0)
    table = table.astype(F32).astype(BF16)
    dep = jnp.zeros((32, L), F32)
    to_scalar = []
    for side in (3, 2, 1, 0):
        for b in range(CAP // L):
            r = side * (CAP // L) + b
            mine, low = onehots(ids_v[side : side + 1, b * L : (b + 1) * L])
            live = (lane + b * L < cnt[side]).astype(F32)
            dep = dep + dot_nt((mine.astype(F32) * live).astype(BF16), low)
            found = dot_nn(table, low)
            pick = [
                jnp.sum(jnp.where(mine, found[32 * m : 32 * m + 32], 0.0), 0, keepdims=True)
                for m in range(4)
            ]
            nums[r : r + 1, :] = (pick[0] * 128.0 + pick[1]).astype(I32)
            nums[ne + r : ne + r + 1, :] = (pick[2] * 128.0 + pick[3]).astype(I32)
    to_scalar = pltpu.make_async_copy(nums, nums_s, sems.at[2])
    to_scalar.start()
    keep[...] = 1.0 - jnp.minimum(dep, 1.0)

    to_scalar.wait()
    pack_loop(cnt, (3, 2), (yu, yd), record_plan(ids, nums_s, xs, xg, xf), bufs)


def pack_first(ids, owners, cnt, st, ge, fb):
    return pl.pallas_call(
        first_body,
        out_shape=[jax.ShapeDtypeStruct((RSGF, CAP), F32)] * 2
        + [jax.ShapeDtypeStruct((E, L), F32)] * 2
        + [
            jax.ShapeDtypeStruct((2 * E, L), F32),
            jax.ShapeDtypeStruct((64, L), I32),
            jax.ShapeDtypeStruct((32, L), F32),
        ],
        in_specs=[spec(HBM)] * 6,
        out_specs=[spec()] * 7,
        scratch_shapes=[
            VMEM((4, CAP), I32),
            VMEM((64, L), I32),
            VMEM((RS, E), F32),
            VMEM((RG, E), F32),
            VMEM((RF, 2 * E), F32),
            SMEM((64, L), I32),
        ]
        + [VMEM((L, L), F32)] * 8
        + [
            pltpu.SemaphoreType.DMA((3,)),
            pltpu.SemaphoreType.DMA((CHUNKS, 2)),
            pltpu.SemaphoreType.DMA((CHUNKS, 1)),
        ]
        + ids_scratch(),
        compiler_params=params(20),
        cost_estimate=LARGE,
        name="pack_gy",
    )(*in_hbm(ids, owners, cnt, st, ge, fb))


def rest_body(
    ids_h, cnt_h, ad_h, xs, xg, xf, nums, xu, xd, yu, yd, ad, x0, x1, nums_s, *rest,
):
    (insem, numsem, cnt, ids, idsem) = rest[12:]
    bufs = buffers(rest[:12])
    to_scalar = pltpu.make_async_copy(nums, nums_s, numsem)
    to_scalar.start()
    chunks = fetch(((ad_h, ad),), insem)
    moved = ids_to_scalar(cnt_h, cnt, ids_h, ids, idsem, range(4))

    def fwd(c, carry):
        x0[at(c), :] = ad[0:L, at(c)].T
        x1[at(c), :] = padded(ad[L:RA, at(c)], L).T
        return carry

    over_chunks(chunks, E // L // CHUNKS, fwd, 4)
    for c in moved:
        c.wait()
    to_scalar.wait()
    faces = record_plan(ids, nums_s, xs, xg, xf)
    elems = (ids, 0, [*faces[0][2], (x0, ADJ0, L), (x1, ADJ0 + L, RA - L)])
    pack_loop(cnt, (1, 0), (xu, xd), (elems, *faces[1:]), bufs)
    pack_loop(cnt, (3, 2), (yu, yd), ((ids, 0, [(x0, 0, L), (x1, L, RA - L)]),), bufs)


def pack_rest(ids, cnt, ad, picked):
    return pl.pallas_call(
        rest_body,
        out_shape=[jax.ShapeDtypeStruct((RALL, CAP), F32)] * 2
        + [jax.ShapeDtypeStruct((RA, CAP), F32)] * 2,
        in_specs=[spec(HBM)] * 3 + [spec()] * 4,
        out_specs=[spec()] * 4,
        scratch_shapes=[VMEM((RA, E), F32)]
        + [VMEM((E, L), F32)] * 2
        + [SMEM((64, L), I32)]
        + [VMEM((L, L), F32)] * 12
        + [pltpu.SemaphoreType.DMA((CHUNKS, 1)), pltpu.SemaphoreType.DMA]
        + ids_scratch(),
        compiler_params=params(22),
        cost_estimate=LARGE,
        name="pack_rest",
    )(*in_hbm(ids, cnt, ad), *picked)


def keep_body(
    owners_h, st_h, ad_h, ge_h, fb_h, keep, st_out, ad_out, ge_out, fb_out,
    owners, st, ad, ge, fb, insem, outsem, sem,
):
    own_copy = pltpu.make_async_copy(owners_h, owners, sem)
    own_copy.start()
    local = (st, ad, ge, fb)
    chunks = fetch(list(zip((st_h, ad_h, ge_h, fb_h), local)), insem, KEEP_PARTS)
    own_copy.wait()
    kept16 = keep[...].astype(BF16)
    back = []

    def scale(g, carry):
        for u in range(8):
            c = g * 8 + u
            mine, low = onehots(owners[pl.ds(c, 1), :])
            k = jnp.sum(jnp.where(mine, dot_nn(kept16, low), 0.0), 0, keepdims=True)
            fb[:, at(c)] = fb[:, at(c)] * k
        for u in range(4):
            c = g * 4 + u
            k = keep[pl.ds(c, 1), :]
            for x in (st, ad, ge):
                x[:, at(c)] = x[:, at(c)] * k
        return carry

    steps = E // L // 4 // KEEP_PARTS
    for q, group in enumerate(chunks):
        for c in group:
            c.wait()
        lax.fori_loop(q * steps, (q + 1) * steps, scale, 0)
        for m, (x, out) in enumerate(zip(local, (st_out, ad_out, ge_out, fb_out))):
            width = x.shape[1] // KEEP_PARTS
            cols = pl.ds(q * width, width)
            back.append(pltpu.make_async_copy(x.at[:, cols], out.at[:, cols], outsem.at[q, m]))
            back[-1].start()
    for c in back:
        c.wait()


def keep_own(owners, st, ad, ge, fb, keep):
    return pl.pallas_call(
        keep_body,
        out_shape=[
            jax.ShapeDtypeStruct((RS, 2 * E), F32),
            jax.ShapeDtypeStruct((RA, 2 * E), F32),
            jax.ShapeDtypeStruct((RG, 2 * E), F32),
            jax.ShapeDtypeStruct((RF, 4 * E), F32),
        ],
        in_specs=[spec(HBM)] * 5 + [spec()],
        out_specs=[spec(HBM)] * 4,
        scratch_shapes=[
            VMEM((64, L), I32),
            VMEM((RS, E), F32),
            VMEM((RA, E), F32),
            VMEM((RG, E), F32),
            VMEM((RF, 2 * E), F32),
            pltpu.SemaphoreType.DMA((KEEP_PARTS, 4)),
            pltpu.SemaphoreType.DMA((KEEP_PARTS, 4)),
            pltpu.SemaphoreType.DMA,
        ],
        compiler_params=params(12),
        cost_estimate=LARGE,
        name="keep_own",
    )(*in_hbm(owners, st, ad, ge, fb), keep)


NB = 256
PER = 4


def split(x):
    hi = x.astype(BF16)
    return hi, (x - hi.astype(F32)).astype(BF16)


def arrive_body(
    part, first_call, speeds, basis, grad, test, lift, *rest,
):
    (xa, xb), rest = rest[:2], rest[2:]
    if first_call:
        st_in, ge_in, fb_in, st_out, ge_out, fb_out, res_out = rest[:7]
        rest = rest[7:]
    else:
        st_in, ge_in, fb_in, res_in, ad_in, st_out, ge_out, fb_out, res_out, ad_out = rest[:10]
        rest = rest[10:]
    wf, w3, tt, lf, ll, vj0, vj1, fh0, fh1, ks, kg, k1, k2, kr, sems = rest

    adj_copies = []
    if not first_call:
        for q, x in enumerate((xa, xb)):
            to = ad_out.at[:, pl.ds(E + (part * 2 + q) * CAP, CAP)]
            adj_copies.append(pltpu.make_async_copy(x.at[pl.ds(ADJ0, RA), :], to, sems.at[10 + q]))
            adj_copies[-1].start()
    wf[...] = jnp.zeros_like(wf)
    for v in range(NV):
        wf[v * NS : (v + 1) * NS, v * QP : v * QP + NQ] = basis[...]
    for c in range(3):
        for k in range(3):
            r = VALS + (c * 3 + k) * QP
            wf[RS + c * NS : RS + (c + 1) * NS, r : r + NQ] = grad[k]
    for r in range(0, 768, L):
        top = wf[0:L, r : r + L].T
        low = wf[L : 2 * L, r : r + L].T
        wide = jnp.concatenate([top, low], 1)[: min(L, WROWS - r)]
        wh, wl = split(wide[:, 0:RSG])
        here = slice(r, min(r + L, WROWS))
        w3[here, 0:RSG] = wh
        w3[here, RSG : 2 * RSG] = wh
        w3[here, 2 * RSG : 3 * RSG] = wl
    lf[...] = jnp.zeros_like(lf)
    lf[0:NA, 0 : 3 * QP] = jnp.zeros((NA, 3 * QP), F32)
    for k in range(3):
        lf[0:NA, k * QP : k * QP + NQ] = test[:, k * NQ : (k + 1) * NQ]
    th, tl = split(lf[0:48, 0 : 3 * QP])
    tt[0:48, :] = th
    tt[48:96, :] = tl
    lf[...] = jnp.zeros_like(lf)
    for v in range(NV):
        lf[v * NFT : (v + 1) * NFT, v * 40 : v * 40 + NA] = lift[...]
    lt = jnp.concatenate([lf[0:L, 0:L].T, lf[0:L, L : 2 * L].T], 0)
    lh, l2 = split(lt[0:208, 0:80])
    ll[0:208, :] = lh
    ll[208:416, :] = l2

    def block(b, rec, d, vj, fh):
        src = slice(b * NB, (b + 1) * NB)
        dst = slice(d * CAP + b * NB, d * CAP + (b + 1) * NB)
        x = rec[0:RSG, src]
        ks[:, dst] = x[0:RS]
        kg[:, dst] = x[RS:RSG]
        f1, f2 = rec[RSG : RSG + RF, src], rec[RSG + RF : RSGF, src]
        k1[:, dst] = f1
        k2[:, dst] = f2
        hi, lo = split(x)
        vj[...] = dot_nn(w3[...], jnp.concatenate([hi, lo, hi], 0))
        for t in range(QP // 16):
            for h in range(NB // L):
                lanes = slice(h * L, (h + 1) * L)

                def part_of(r):
                    return vj[r + 16 * t : r + 16 * t + 16, lanes]

                jac = [[part_of(VALS + (c * 3 + k) * QP) for k in range(3)] for c in range(3)]
                flux = []
                for v in range(NV):
                    u = part_of(v * QP)
                    flux.append(u + u * (0.5 * jnp.tanh(u)))
                for k in range(3):
                    k1_, k2_ = (k + 1) % 3, (k + 2) % 3
                    cof = []
                    for c in range(3):
                        c1, c2 = (c + 1) % 3, (c + 2) % 3
                        cof.append(jac[c1][k1_] * jac[c2][k2_] - jac[c1][k2_] * jac[c2][k1_])
                    for v in range(NV):
                        w = cof[0] * speeds[0, v] + cof[1] * speeds[1, v] + cof[2] * speeds[2, v]
                        fhi, flo = split(w * flux[v])
                        r = k * QP + 16 * t
                        wide = slice(v * NB + h * L, v * NB + (h + 1) * L)
                        fh[0, r : r + 16, wide] = fhi
                        fh[1, r : r + 16, wide] = flo
        fs = jnp.concatenate([f1 + f2, jnp.zeros((80 - RF, NB), F32)], 0)
        shi, slo = split(fs)
        m1 = dot_nn(ll[...], shi)
        lifted = m1[0:208] + m1[208:416] + dot_nn(ll[0:208, :], slo)
        d1 = dot_nn(tt[...], fh[0])
        d2 = dot_nn(tt[0:48, :], fh[1])
        volume = d1[0:40] + d1[48:88] + d2[0:40]
        for v in range(NV):
            total = volume[:, v * NB : (v + 1) * NB] + lifted[40 * v : 40 * v + 40]
            kr[NA * v : NA * (v + 1), dst] = total[0:NA]

    copies = []

    def send(first, width):
        here = pl.ds(first, width)
        for x, out, base in (
            (ks, st_out, E + part * 2 * CAP),
            (kg, ge_out, E + part * 2 * CAP),
            (k1, fb_out, 2 * E + part * 2 * CAP),
            (k2, fb_out, 3 * E + part * 2 * CAP),
            (kr, res_out, part * 2 * CAP),
        ):
            to = out.at[:, pl.ds(base + first, width)]
            copies.append(pltpu.make_async_copy(x.at[:, here], to, sems.at[len(copies)]))
            copies[-1].start()

    for d, rec in enumerate((xa, xb)):
        for b in range(CAP // NB):
            block(b, rec, d, *((vj0, fh0), (vj1, fh1))[b % 2])
            if (b + 1) % PER == 0:
                send(d * CAP + (b + 1 - PER) * NB, PER * NB)
    for c in copies + adj_copies:
        c.wait()


def arrive(part, weights, pieces, outs):
    speeds, basis, grad, test, lift = weights
    first_call = len(outs) == 3
    shapes = [
        jax.ShapeDtypeStruct((RS, 2 * E), F32),
        jax.ShapeDtypeStruct((RG, 2 * E), F32),
        jax.ShapeDtypeStruct((RF, 4 * E), F32),
        jax.ShapeDtypeStruct((RA, E), F32),
    ] + [jax.ShapeDtypeStruct((RA, 2 * E), F32)] * (len(outs) == 5)
    return pl.pallas_call(
        functools.partial(arrive_body, part, first_call),
        out_shape=shapes,
        in_specs=[spec(SMEM)] + [spec()] * (4 + len(pieces)) + [spec(HBM)] * len(outs),
        out_specs=[spec(HBM)] * len(shapes),
        input_output_aliases={5 + len(pieces) + i: i for i in range(len(outs))},
        scratch_shapes=[
            VMEM((256, 768), F32),
            VMEM((WROWS, 3 * RSG), BF16),
            VMEM((96, 3 * QP), BF16),
            VMEM((208, 256), F32),
            VMEM((416, 80), BF16),
            VMEM((WROWS, NB), F32),
            VMEM((WROWS, NB), F32),
            VMEM((2, 3 * QP, NV * NB), BF16),
            VMEM((2, 3 * QP, NV * NB), BF16),
            VMEM((RS, 2 * CAP), F32),
            VMEM((RG, 2 * CAP), F32),
            VMEM((RF, 2 * CAP), F32),
            VMEM((RF, 2 * CAP), F32),
            VMEM((RA, 2 * CAP), F32),
            pltpu.SemaphoreType.DMA((12,)),
        ],
        compiler_params=params(24),
        cost_estimate=SMALL if part else SMALL,
        name="arrive_gy" if part else "arrive_gx",
    )(speeds, basis, grad, test, lift, *pieces, *outs)


def place_body(part, a, b, ad_in, ad_out, sems):
    copies = [
        pltpu.make_async_copy(src, ad_out.at[:, pl.ds(E + (part * 2 + q) * CAP, CAP)], sems.at[q])
        for q, src in enumerate((a, b))
    ]
    for c in copies:
        c.start()
    for c in copies:
        c.wait()


def place(part, pieces, ad_out):
    return pl.pallas_call(
        functools.partial(place_body, part),
        out_shape=jax.ShapeDtypeStruct((RA, 2 * E), F32),
        in_specs=[spec(), spec(), spec(HBM)],
        out_specs=spec(HBM),
        input_output_aliases={2: 0},
        scratch_shapes=[pltpu.SemaphoreType.DMA((2,))],
        compiler_params=params(4),
        cost_estimate=SMALL,
        name="place_gy" if part else "place_gx",
    )(*pieces, ad_out)


def in_hbm(*arrays):
    return [pltpu.with_memory_space_constraint(a, HBM) for a in arrays]


def after(value, done):
    return lax.optimization_barrier((value, done))


def exchange(axis, toward_high, toward_low):
    size = lax.axis_size(axis)
    up = [(i, i + 1) for i in range(size - 1)]
    down = [(j, i) for i, j in up]
    return lax.ppermute(toward_high, axis, up), lax.ppermute(toward_low, axis, down)


def per_device(
    state, adjoint, geometry, face_blocks, face_elem, move_ids, move_counts,
    basis, geo_grad, test_grad, lift, speeds,
):
    ids = move_ids
    owners = face_elem.reshape(2 * E // L, L)
    yu, yd, *picked, keep = pack_first(ids, owners, move_counts, state, geometry, face_blocks)
    in_y = exchange("gy", yu, yd)
    xu, xd, ayu, ayd = pack_rest(ids, move_counts, adjoint, picked)
    in_x = exchange("gx", xu, xd)
    keep, _ = after(keep, (xu, xd))
    state_out, adjoint_out, geometry_out, faces_out = keep_own(
        owners, state, adjoint, geometry, face_blocks, keep
    )
    (ayu, ayd, in_y), _ = after((ayu, ayd, in_y), faces_out)
    ad_y = exchange("gy", ayu, ayd)
    weights = (speeds, basis.T, geo_grad.transpose(0, 2, 1), test_grad, lift.T)
    outs = arrive(1, weights, in_y, (state_out, geometry_out, faces_out))
    outs = arrive(0, weights, in_x, (*outs, adjoint_out))
    state_out, geometry_out, faces_out, residual, adjoint_out = outs
    ad_y, _ = after(ad_y, residual)
    adjoint_out = place(1, ad_y, adjoint_out)
    return state_out, adjoint_out, geometry_out, faces_out, residual


def solution(mesh):
    cols = P(None, ("gx", "gy"))
    flat = P(("gx", "gy"))
    return jax.shard_map(
        per_device,
        mesh=mesh,
        in_specs=(cols, cols, cols, cols, flat, P(("gx", "gy"), None), flat, P(), P(), P(), P(), P()),
        out_specs=(cols, cols, cols, cols, cols),
        check_vma=False,
    )
```
